256 devices in a mesh: seq: 128 (over y_lo, x, z, core), req: 2 (over y_hi).
Axes of the slice: x: 4, y: 4 (y_hi: 2, y_lo: 2; y = y_hi * 2 + y_lo), z: 8, core: 2. Of those that a mesh axis runs over, the one named last changes fastest.
Arguments:
- tokens: bfloat16 [16384, 2048], P('seq'), may hold values from -6 to 6
- norm_gain: float32 [2048], replicated, may hold values from 0.5 to 1.5
- w_query: bfloat16 [2048, 1024], P(None, 'req'), as said below
- key_projection: bfloat16 [2048, 512], P(None, 'req')
- value_projection: bfloat16 [2048, 512], P(None, 'req'), may hold values from -0.125 to 0.125
- w_out: bfloat16 [1024, 2048], P('req'), may hold values from -0.1875 to 0.1875
- lengths: int32 [4], replicated, may hold values from 1 to 10922, 16384 in all
- block_split: int32 [128], replicated, may hold values from 0 to 127, each once
- page_slot: int32 [512], replicated, may hold values from 0 to 1023, as said below
Outputs:
- hidden: bfloat16 [16384, 2048], P(('seq', 'req'))
- key_value_cache: bfloat16 [1024, 2, 32, 512], P('seq', None, None, 'req')
The draws below stay inside these ranges and needn't reach their ends.
Inputs may be any that keep to these rules, and one draw needn't show every extreme that they name: block_split is a permutation; index i of seq holds block block_split[i] and its mirror. `page_slot`: distinct slots; slot s lies on index s // 8 of seq. `w_query`: a projection scaled like 2 / sqrt(2048).
All inputs are finite; a program needn't handle non-finite values.
Results may differ from the reference program's by a relative error of at most 0.014.
The reference program's roundings to bfloat16 on the way count: a program that leaves them out, or rounds other values in their place, can miss the bound.
Values may be sent and summed in bfloat16 or wider, within the bound.
A program may use at most 128 MiB of HBM per device.

```python
import math
import jax
import jax.numpy as jnp
import numpy as np
from jax import lax

MODEL_WIDTH = 2048
QUERY_HEADS = 8
KEY_VALUE_HEADS = 4
HEAD_SIZE = 128
TOKENS_PER_SEQ = 128
REQS = 4
PAGE_TOKENS = 32
TOTAL_TOKENS = 16384
PAGES_PER_SEQ = 8
NPAGES = 512
N_SEQ = 128


def query_key_pair(key):
    base_key = jax.random.fold_in(key, 11)
    first_key, second_random_key = jax.random.split(base_key, 2)
    spread_values = 2.0 / math.sqrt(MODEL_WIDTH)
    query_matrix = jax.random.normal(first_key, (MODEL_WIDTH, QUERY_HEADS * HEAD_SIZE), jnp.float32) * spread_values
    noise_sample = jax.random.normal(second_random_key, (MODEL_WIDTH, KEY_VALUE_HEADS * HEAD_SIZE), jnp.float32) * spread_values
    key_weight = noise_sample
    return (query_matrix.astype(jnp.bfloat16), key_weight.astype(jnp.bfloat16))


def draw_w_query(key, part):
    return query_key_pair(key)[0]


def draw_key_projection(key, part):
    return query_key_pair(key)[1]


def draw_page_slot(key, part):
    base_key = jax.random.fold_in(key, 29)
    heat_key, noise_key, order_key, page_key = jax.random.split(base_key, 4)
    slot_total = N_SEQ * PAGES_PER_SEQ
    levels = jax.random.randint(heat_key, (N_SEQ,), 0, 4)
    heat = levels * levels * 400
    noise_sample = jax.random.randint(noise_key, (N_SEQ, PAGES_PER_SEQ), 0, 2000)
    scores = (heat[:, None] + noise_sample).reshape(slot_total)
    scores = scores.at[slot_total - 1].set(10000)
    ranks = scores * slot_total + jax.random.permutation(order_key, slot_total)
    chosen = jnp.argsort(-ranks, stable=True)[:NPAGES]
    shuffle = jax.random.permutation(page_key, NPAGES)
    return chosen[shuffle].astype(jnp.int32)


def level_of(stream_key, shape, pieces, least, largest):
    def one(dim, blocks):
        steps = jax.random.uniform(jax.random.fold_in(jax.random.fold_in(stream_key, 6), dim), (blocks,), jnp.float32, least / len(pieces), largest / len(pieces))
        return jnp.repeat(jnp.exp(steps), shape[dim] // blocks).reshape((-1,) + (1,) * (len(shape) - dim - 1))

    loudness = one(*pieces[0])
    for cut in pieces[1:]:
        loudness = loudness * one(*cut)
    return loudness


def profile(number_of, total, bound, lean):
    loads = [(1 << 20) // math.isqrt(standing ** lean) + 1 for standing in range(2, number_of + 1)]
    rest, given = total - bound - (number_of - 1), [1] * (number_of - 1)
    while rest > 0:
        movable = [i for i in range(number_of - 1) if given[i] < bound]
        whole, remaining = sum([loads[i] for i in movable]), rest
        for i in movable:
            addition = min(bound - given[i], max(1, remaining * loads[i] // whole), rest)
            given[i] = given[i] + addition
            rest = rest - addition
    return np.array([bound] + given)


def ragged(stream_key, number_of, total, most, skew):
    if number_of == 2:
        one = jax.random.randint(stream_key, (), max(1, total - most), min(most, total - 1) + 1)
        return jnp.stack([one, total - one])
    tallies = jnp.asarray(profile(number_of, total, most, skew), jnp.int32)
    twos = (number_of - 1) // 2
    source_of, receiver = tallies[1:1 + 2 * twos:2], tallies[2:2 + 2 * twos:2]
    margin = jnp.minimum(source_of - 1, most - receiver)
    passed = jax.random.randint(jax.random.fold_in(stream_key, 1), (twos,), 0, 1 << 20) % (margin + 1)
    tallies = tallies.at[1:1 + 2 * twos:2].set(source_of - passed).at[2:2 + 2 * twos:2].set(receiver + passed)
    return tallies[jax.random.permutation(jax.random.fold_in(stream_key, 2), number_of)]


def bell_draw(rng, dims, spread, most, shards=(), held_as=jnp.bfloat16):
    level = level_of(rng, dims, shards, -0.22, 0.18) if shards else 1.0
    values = jax.random.normal(rng, dims, jnp.float32) * spread * level
    return jnp.minimum(jnp.maximum(values, -most), most).astype(held_as)


def setup_inputs(seed: int = 0) -> dict:
    key_list = jax.random.split(jax.random.key(seed), 10)
    return {
        "tokens": bell_draw(key_list[0], (TOTAL_TOKENS, MODEL_WIDTH), 1.0, 6.0, ((0, 128),)),
        "norm_gain": jnp.clip(1.0 + 0.1 * jax.random.normal(key_list[1], (MODEL_WIDTH,), jnp.float32), 0.5, 1.5),
        "w_query": draw_w_query(jax.random.fold_in(key_list[9], 71), 0),
        "key_projection": draw_key_projection(jax.random.fold_in(key_list[9], 71), 0),
        "value_projection": bell_draw(key_list[4], (MODEL_WIDTH, KEY_VALUE_HEADS * HEAD_SIZE), MODEL_WIDTH ** -0.5, 0.125, ((1, 2),)),
        "w_out": bell_draw(key_list[5], (QUERY_HEADS * HEAD_SIZE, MODEL_WIDTH), (QUERY_HEADS * HEAD_SIZE) ** -0.5, 0.1875, ((0, 2),)),
        "lengths": ragged(key_list[6], REQS, TOTAL_TOKENS, 2 * TOTAL_TOKENS // 3, 2).astype(jnp.int32),
        "block_split": jax.random.permutation(key_list[7], N_SEQ).astype(jnp.int32),
        "page_slot": draw_page_slot(jax.random.fold_in(key_list[9], 71), 0),
    }


theta_base = 1000000.0
norm_eps = 1e-05
far_below = -1e+30

def rotary_rows(heads, offset_list):
    half_width = heads.shape[-1] // 2
    exponent = jnp.arange(half_width, dtype=jnp.float32) * (2.0 / heads.shape[-1])
    inv_freq = jnp.power(theta_base, -exponent)
    angle = offset_list.astype(jnp.float32)[:, None] * inv_freq[None, :]
    cosine = jnp.concatenate([jnp.cos(angle), jnp.cos(angle)], -1)[:, None, :]
    sine = jnp.concatenate([jnp.sin(angle), jnp.sin(angle)], -1)[:, None, :]
    rolled = jnp.concatenate([-heads[..., half_width:], heads[..., :half_width]], -1)
    return heads * cosine + rolled * sine

def slot_positions(block_split, lengths, total_rows, shard_rows):
    row_ids = jnp.arange(total_rows, dtype=jnp.int32)
    half_rows = shard_rows // 2
    cycle_size = block_split.shape[0]
    owner_dev = row_ids // shard_rows
    device_ids = jnp.arange(cycle_size, dtype=jnp.int32)
    first_block = lax.optimization_barrier(jnp.sum(jnp.where(owner_dev[:, None] == device_ids[None, :], block_split[None, :], 0), 1)).astype(jnp.int32)
    block_ids = jnp.where(row_ids % shard_rows < half_rows, first_block, 2 * cycle_size - 1 - first_block)
    position = (block_ids * half_rows + row_ids % half_rows).astype(jnp.int32)
    request_ends = jnp.cumsum(lengths).astype(jnp.int32)
    request_begins = (request_ends - lengths).astype(jnp.int32)
    request = lax.optimization_barrier(jnp.sum((position[:, None] >= request_ends[None, :]).astype(jnp.int32), 1)).astype(jnp.int32)
    prompt_ids = jnp.arange(lengths.shape[0], dtype=jnp.int32)
    begins = lax.optimization_barrier(jnp.sum(jnp.where(request[:, None] == prompt_ids[None, :], request_begins[None, :], 0), 1)).astype(jnp.int32)
    return (position, request, (position - begins).astype(jnp.int32))

def reference(tokens, norm_gain, w_query, key_projection, value_projection, w_out, lengths, block_split, page_slot):
    position, request, offset_list = slot_positions(block_split, lengths, TOTAL_TOKENS, TOKENS_PER_SEQ)
    widened = tokens.astype(jnp.float32)
    normalized_input = (widened * lax.rsqrt(lax.optimization_barrier(jnp.mean(widened * widened, -1, keepdims=True)) + norm_eps) * norm_gain).astype(jnp.bfloat16)
    query_rotated = rotary_rows(jnp.dot(normalized_input, w_query, preferred_element_type=jnp.float32).reshape(TOTAL_TOKENS, QUERY_HEADS, HEAD_SIZE), offset_list).astype(jnp.bfloat16)
    key_matrix_rows = rotary_rows(jnp.dot(normalized_input, key_projection, preferred_element_type=jnp.float32).reshape(TOTAL_TOKENS, KEY_VALUE_HEADS, HEAD_SIZE), offset_list).astype(jnp.bfloat16)
    value_matrix_rows = jnp.dot(normalized_input, value_projection, preferred_element_type=jnp.float32).astype(jnp.bfloat16)
    group_width = QUERY_HEADS // KEY_VALUE_HEADS
    scale_factor = 1.0 / math.sqrt(HEAD_SIZE)
    key_wide = key_matrix_rows.astype(jnp.float32)
    value_widened = value_matrix_rows.astype(jnp.float32).reshape(TOTAL_TOKENS, KEY_VALUE_HEADS, HEAD_SIZE)
    query_block_list = query_rotated.astype(jnp.float32).reshape(N_SEQ, TOKENS_PER_SEQ, KEY_VALUE_HEADS, group_width, HEAD_SIZE)
    block_pos = position.reshape(N_SEQ, TOKENS_PER_SEQ)
    block_req = request.reshape(N_SEQ, TOKENS_PER_SEQ)

    def attend_block(item):
        query_block, query_pos, query_req = item
        scores = jnp.einsum('qhgd,khd->hgqk', query_block, key_wide, precision=lax.Precision.HIGHEST) * scale_factor
        visible = (request[None, :] == query_req[:, None]) & (position[None, :] <= query_pos[:, None])
        scores = jnp.where(visible[None, None], scores, far_below)
        top_score = lax.optimization_barrier(jnp.max(scores, -1, keepdims=True))
        raised = jnp.where(visible[None, None], jnp.exp(scores - top_score), 0.0)
        denominator = lax.optimization_barrier(jnp.sum(raised, -1))
        rounded = lax.optimization_barrier(raised.astype(jnp.bfloat16)).astype(jnp.float32)
        result = jnp.einsum('hgqk,khd->hgqd', rounded, value_widened, precision=lax.Precision.HIGHEST)
        result = result / denominator[..., None]
        return jnp.transpose(result, (2, 0, 1, 3)).reshape(TOKENS_PER_SEQ, QUERY_HEADS * HEAD_SIZE)
    context = lax.map(attend_block, (query_block_list, block_pos, block_req)).reshape(TOTAL_TOKENS, QUERY_HEADS * HEAD_SIZE).astype(jnp.bfloat16)
    hidden = (tokens.astype(jnp.float32) + jnp.dot(context, w_out, preferred_element_type=jnp.float32)).astype(jnp.bfloat16)
    slot_ids = page_slot[position // PAGE_TOKENS]
    target_rows = slot_ids * PAGE_TOKENS + position % PAGE_TOKENS
    paired_rows = jnp.stack([key_matrix_rows.reshape(TOTAL_TOKENS, KEY_VALUE_HEADS * HEAD_SIZE), value_matrix_rows], 1)
    flattened = jnp.zeros((N_SEQ * PAGES_PER_SEQ * PAGE_TOKENS, 2, KEY_VALUE_HEADS * HEAD_SIZE), jnp.bfloat16).at[target_rows].set(paired_rows)
    key_value_cache = jnp.transpose(flattened.reshape(N_SEQ * PAGES_PER_SEQ, PAGE_TOKENS, 2, KEY_VALUE_HEADS * HEAD_SIZE), (0, 2, 1, 3))
    return (hidden, key_value_cache)
```

```python
import math

import jax
import jax.numpy as jnp
from jax import lax
from jax.experimental import pallas as pl
from jax.experimental.pallas import tpu as pltpu
from jax.sharding import PartitionSpec as P

MESH = pl.DeviceIdType.MESH
ANY = pl.BlockSpec(memory_space=pl.ANY)
HBM = pl.BlockSpec(memory_space=pltpu.HBM)
VMEM = pl.BlockSpec(memory_space=pltpu.VMEM)
SMEM = pl.BlockSpec(memory_space=pltpu.SMEM)

NY, NX, NZ, NC = 2, 4, 8, 2
NSEQ = NY * NX * NZ * NC
NXY = NX * NY
HEAD = 128
BLOCK = 64
ROWS = 128
PAGE = 32
SLOTS = 8
WIDTH = 2048
QCOLS = 512
KCOLS = 256
THETA = 1000000.0
EPS = 1e-05
FAR = -1e30
FLOOR = -1e29
SCALE2 = math.log2(math.e) / math.sqrt(HEAD)
MIB = 1 << 20
BF16 = jnp.bfloat16
F32 = jnp.float32

STEP = 8
QUAD = 4
KEYS = STEP * BLOCK
LANES = QUAD * 2 * BLOCK
GROUPS = 2 * NXY // QUAD

T_IDX = 0
T_BLK = T_IDX + 64
T_QIDX = T_BLK + 64 + STEP
T_QBLK = T_QIDX + 2 * NXY
T_LO = T_QBLK + 2 * NXY
T_STEPS = T_LO + GROUPS
T_BEGIN = T_STEPS + GROUPS
T_PAGE = T_BEGIN + 4


def coords(d):
    return d // 64, (d // 16) % NX, (d // 2) % NZ, d % 2


def index_of(y, x, z, c):
    return ((y * NX + x) * NZ + z) * NC + c


def plane(y, x, z, c):
    return [
        ((x + i) % NX, y if j == 0 else 1 - y, index_of(y if j == 0 else 1 - y, (x + i) % NX, z, c))
        for j in range(NY)
        for i in range(NX)
    ]


NODES = [(0, 0)]
for _k in (1, 2, 3):
    NODES += [(1, -_k), (1, _k), (0, -_k), (0, _k)]
NODES += [(1, 4), (0, 4)]


def passed_on(own, dz):
    out = []
    if -3 < dz <= 0 or (dz == -3 and own):
        out.append(("up", dz - 1))
    if 0 <= dz < 3 or (dz == 3 and not own):
        out.append(("down", dz + 1))
    return [(to, 4 if abs(to_dz) == 4 else to_dz) for to, to_dz in out]


def gather_kernel(
    tok_hbm, gain_ref, wq_hbm, wk_hbm, wv_hbm, cos_ref, sin_ref, kvall, qall,
    tok, wq, wk, wv, normed, acc, kv, q, load_sem, send_sem, recv_sem, local_sem,
):
    d, r = lax.axis_index("seq"), lax.axis_index("req")
    y, x, z, c = coords(d)
    loads = [pltpu.make_async_copy(tok_hbm, tok, load_sem.at[0])]
    for k in range(4):
        rows = pl.ds(512 * k, 512)
        for n, (src, dst) in enumerate(((wq_hbm, wq), (wk_hbm, wk), (wv_hbm, wv))):
            loads.append(
                pltpu.make_async_copy(src.at[rows], dst.at[rows], load_sem.at[1 + 3 * k + n])
            )
    for copy in loads:
        copy.start()
    near = {
        "sib": index_of(y, x, z, 1 - c),
        "up": index_of(y, x, (z + 1) % NZ, c),
        "down": index_of(y, x, (z + NZ - 1) % NZ, c),
    }
    peers = plane(y, x, z, c)
    barrier = pltpu.get_barrier_semaphore()
    everyone = list(near.values()) + [peer[2] for peer in peers[1:]]
    for peer in everyone:
        pl.semaphore_signal(barrier, inc=1, device_id=(peer, r), device_id_type=MESH)

    loads[0].wait()
    wide = tok[...].astype(F32)
    inv = lax.rsqrt(jnp.mean(wide * wide, -1, keepdims=True) + EPS)
    normed[...] = (wide * inv * gain_ref[...]).astype(BF16)
    for k in range(4):
        for copy in loads[1 + 3 * k : 4 + 3 * k]:
            copy.wait()
        rows = slice(512 * k, 512 * (k + 1))
        part = normed[:, rows]
        for cols, weights in ((slice(0, 512), wq), (slice(512, 768), wk), (slice(768, 1024), wv)):
            value = jnp.dot(part, weights[rows, :], preferred_element_type=F32)
            if k == 0:
                acc[:, cols] = value
            else:
                acc[:, cols] += value
    cosine, sine = cos_ref[...], sin_ref[...]
    for h in range(6):
        u = acc[:, HEAD * h : HEAD * (h + 1)]
        turned = (u * cosine + pltpu.roll(u, HEAD // 2, 1) * sine).astype(BF16)
        if h < 4:
            q[h // 2, :, HEAD * (h % 2) : HEAD * (h % 2 + 1)] = turned
        else:
            kv[h - 4, 0] = turned
    for g in range(2):
        kv[g, 1] = acc[:, 768 + HEAD * g : 768 + HEAD * (g + 1)].astype(BF16)
    pl.semaphore_wait(barrier, len(everyone))

    flying = {}

    def send(name, n, src, dst, to):
        copy = pltpu.make_async_remote_copy(
            src_ref=src,
            dst_ref=dst,
            send_sem=send_sem.at[n],
            recv_sem=recv_sem.at[n],
            device_id=(to, r),
            device_id_type=MESH,
        )
        copy.start()
        flying[name] = copy

    def shard(own, dz):
        return kvall.at[(z + dz + NZ) % NZ, c, y if own else 1 - y]

    def relay(own, dz):
        here = shard(own, dz)
        src = kv.at[y] if (own, dz) == (1, 0) else here
        for to, far in passed_on(own, dz):
            send((own, far), NODES.index((own, far)), src, here, near[to])
        n = len(NODES) + 8 * own + dz % NZ
        send(("s", own, dz), n, src, here, near["sib"])

    relay(1, 0)
    send((0, 0), 0, kv.at[1 - y], shard(1, 0), peers[NX][2])
    for n, (px, py, peer) in enumerate(peers):
        if n:
            send(("q", n), len(NODES) + 15 + n, q.at[py], qall.at[x, y], peer)
    keep = [
        pltpu.make_async_copy(kv.at[y], shard(1, 0), local_sem.at[0]),
        pltpu.make_async_copy(q.at[y], qall.at[x, y], local_sem.at[1]),
    ]
    for copy in keep:
        copy.start()
    for node in NODES:
        flying[node].wait_recv()
        relay(*node)
    for name, copy in flying.items():
        if name[0] in ("s", "q"):
            copy.wait_recv()
    for copy in flying.values():
        copy.wait_send()
    for copy in keep:
        copy.wait()


def gather(tokens, gain, wq, wk, wv, cosine, sine):
    count = len(NODES) + 16 + NXY - 1
    return pl.pallas_call(
        gather_kernel,
        out_shape=(
            jax.ShapeDtypeStruct((NZ, NC, NY, 2, ROWS, HEAD), BF16),
            jax.ShapeDtypeStruct((NX, NY, ROWS, 2 * HEAD), BF16),
        ),
        in_specs=[HBM, VMEM, HBM, HBM, HBM, VMEM, VMEM],
        out_specs=(ANY, ANY),
        scratch_shapes=[
            pltpu.VMEM((ROWS, WIDTH), BF16),
            pltpu.VMEM((WIDTH, QCOLS), BF16),
            pltpu.VMEM((WIDTH, KCOLS), BF16),
            pltpu.VMEM((WIDTH, KCOLS), BF16),
            pltpu.VMEM((ROWS, WIDTH), BF16),
            pltpu.VMEM((ROWS, 1024), F32),
            pltpu.VMEM((2, 2, ROWS, HEAD), BF16),
            pltpu.VMEM((2, ROWS, 2 * HEAD), BF16),
            pltpu.SemaphoreType.DMA((13,)),
            pltpu.SemaphoreType.DMA((count,)),
            pltpu.SemaphoreType.DMA((count,)),
            pltpu.SemaphoreType.DMA((2,)),
        ],
        compiler_params=pltpu.CompilerParams(
            collective_id=1, has_side_effects=True, vmem_limit_bytes=32 * MIB
        ),
        name="gather",
    )(tokens, gain, wq, wk, wv, cosine, sine)


def attend_kernel(
    table, q_ref, kv_ref, o_ref, lse_ref, pages_ref, keys, values, queries, acc, top, total
):
    def block_rows(part, at):
        rows = kv_ref[at // 2, part, pl.ds(at % 2 * 2, 2)]
        return rows.reshape(BLOCK, HEAD)

    def sort_pair(n, _):
        one, two = table[T_IDX + 2 * n], table[T_IDX + 2 * n + 1]
        at = pl.multiple_of(n * 2 * BLOCK, 2 * BLOCK)
        keys[pl.ds(at, BLOCK), :] = block_rows(0, one)
        keys[pl.ds(at + BLOCK, BLOCK), :] = block_rows(0, two)
        pair = jnp.concatenate([block_rows(1, one), block_rows(1, two)], 0)
        values[:, pl.ds(at, 2 * BLOCK)] = jnp.transpose(pair)
        return 0

    lax.fori_loop(0, 32, sort_pair, 0, unroll=4)
    keys[64 * BLOCK :, :] = jnp.zeros((KEYS, HEAD), BF16)
    values[:, 64 * BLOCK :] = jnp.zeros((HEAD, KEYS), BF16)

    def sort_query(n, _):
        at = table[T_QIDX + n]
        rows = q_ref[at // 2, at % 2]
        to = pl.multiple_of(n * 2 * BLOCK, 2 * BLOCK)
        queries[pl.ds(to, BLOCK), :] = rows[:, :HEAD]
        queries[pl.ds(to + BLOCK, BLOCK), :] = rows[:, HEAD:]
        return 0

    lax.fori_loop(0, 2 * NXY, sort_query, 0, unroll=4)

    def pick(n, _):
        at = table[T_PAGE + n]
        for part in range(2):
            pages_ref[n // SLOTS, n % SLOTS, part] = kv_ref[at // 4, part, at % 4]
        return 0

    lax.fori_loop(0, NXY * SLOTS, pick, 0, unroll=4)

    lane = lax.broadcasted_iota(jnp.int32, (1, 2 * BLOCK), 1) % BLOCK
    inner = lax.broadcasted_iota(jnp.int32, (BLOCK, LANES), 0)

    def group(m, _):
        pos = jnp.concatenate(
            [table[T_QBLK + QUAD * m + j] * BLOCK + lane for j in range(QUAD)], 1
        )
        first = jnp.zeros_like(pos)
        for k in range(1, 4):
            begin = table[T_BEGIN + k]
            first = jnp.where(pos >= begin, begin, first)
        mine = queries[pl.ds(pl.multiple_of(m * LANES, LANES), LANES), :]
        lo = table[T_LO + m]
        top[...] = jnp.full_like(top, FLOOR)
        total[...] = jnp.zeros_like(total)
        acc[...] = jnp.zeros_like(acc)

        def step(n, _):
            rank = lo + n * STEP
            at = pl.multiple_of(rank * BLOCK, 2 * BLOCK)
            s = lax.dot_general(
                keys[pl.ds(at, KEYS), :], mine, (((1,), (1,)), ((), ())), preferred_element_type=F32
            )
            pieces = []
            for j in range(STEP):
                base = table[T_BLK + rank + j] * BLOCK
                visible = (inner >= first - base) & (inner <= pos - base)
                pieces.append(jnp.where(visible, s[j * BLOCK : (j + 1) * BLOCK], FAR))
            s = jnp.concatenate(pieces, 0)
            before = top[...]
            higher = jnp.maximum(before, jnp.max(s, 0, keepdims=True))
            e = jnp.exp2((s - higher) * SCALE2)
            fade = jnp.exp2((before - higher) * SCALE2)
            top[...] = higher
            total[...] = total[...] * fade + jnp.sum(e, 0, keepdims=True)
            acc[...] = acc[...] * fade + jnp.dot(
                values[:, pl.ds(at, KEYS)], e.astype(BF16), preferred_element_type=F32
            )
            return 0

        lax.fori_loop(0, table[T_STEPS + m], step, 0)
        seen = total[...] > 0.0
        safe = jnp.where(seen, total[...], 1.0)
        lse = jnp.where(seen, top[...] * SCALE2 + jnp.log2(safe), FAR)
        inverse = 1.0 / safe
        for j in range(QUAD):
            at = table[T_QIDX + QUAD * m + j]
            cols = slice(j * 2 * BLOCK, (j + 1) * 2 * BLOCK)
            out = jnp.transpose(acc[:, cols] * inverse[:, cols]).astype(BF16)
            o_ref[at // 2, at % 2, :, :HEAD] = out[:BLOCK]
            o_ref[at // 2, at % 2, :, HEAD:] = out[BLOCK:]
            lse_ref[at // 2, at % 2] = jnp.broadcast_to(lse[:, cols], (8, 2 * BLOCK))
        return 0

    lax.fori_loop(0, GROUPS, group, 0)


def attend(table, q, kv):
    return pl.pallas_call(
        attend_kernel,
        in_specs=[SMEM, VMEM, VMEM],
        out_specs=(VMEM, VMEM, VMEM),
        out_shape=(
            jax.ShapeDtypeStruct((NXY, 2, BLOCK, 2 * HEAD), BF16),
            jax.ShapeDtypeStruct((NXY, 2, 8, 2 * BLOCK), F32),
            jax.ShapeDtypeStruct((NXY, SLOTS, 2, PAGE, HEAD), BF16),
        ),
        scratch_shapes=[
            pltpu.VMEM((64 * BLOCK + KEYS, HEAD), BF16),
            pltpu.VMEM((HEAD, 64 * BLOCK + KEYS), BF16),
            pltpu.VMEM((2 * NXY * 2 * BLOCK, HEAD), BF16),
            pltpu.VMEM((HEAD, LANES), F32),
            pltpu.VMEM((1, LANES), F32),
            pltpu.VMEM((1, LANES), F32),
        ],
        compiler_params=pltpu.CompilerParams(vmem_limit_bytes=32 * MIB),
        name="attend",
    )(table, q, kv)


CHUNK = 512
CHUNKS = WIDTH // CHUNK


def finish_kernel(
    column, o_ref, lse_ref, pages_ref, w_ref, tok_ref, out_ref, cache_ref,
    held, lses, fetched, weights, tok, context, mine, outgoing, incoming, send_sem, recv_sem, local_sem,
):
    d, r = lax.axis_index("seq"), lax.axis_index("req")
    y, x, z, c = coords(d)
    partner = 1 - r
    local = [
        pltpu.make_async_copy(o_ref.at[x * NY + y], held.at[x, y], local_sem.at[0]),
        pltpu.make_async_copy(lse_ref.at[x * NY + y], lses.at[x, y], local_sem.at[1]),
        pltpu.make_async_copy(w_ref, weights, local_sem.at[2]),
        pltpu.make_async_copy(tok_ref.at[pl.ds(r * BLOCK, BLOCK)], tok, local_sem.at[3]),
        pltpu.make_async_copy(pages_ref.at[x * NY + y], fetched.at[x, y], local_sem.at[4]),
    ]
    for copy in local:
        copy.start()
    peers = plane(y, x, z, c)
    barrier = pltpu.get_barrier_semaphore()
    for _, _, peer in peers[1:]:
        pl.semaphore_signal(barrier, inc=1, device_id=(peer, r), device_id_type=MESH)
    pl.semaphore_signal(barrier, inc=1, device_id=(d, partner), device_id_type=MESH)
    pl.semaphore_wait(barrier, NXY)

    def send(n, src, dst, to):
        copy = pltpu.make_async_remote_copy(
            src_ref=src,
            dst_ref=dst,
            send_sem=send_sem.at[n],
            recv_sem=recv_sem.at[n],
            device_id=to,
            device_id_type=MESH,
        )
        copy.start()
        return copy

    def to_plane(first, src, dst):
        return [
            send(first + n, src.at[px * NY + py], dst.at[x, y], (peer, r))
            for n, (px, py, peer) in enumerate(peers[1:])
        ]

    parts = to_plane(0, lse_ref, lses) + to_plane(7, o_ref, held)
    for copy in local:
        copy.wait()
    for copy in parts:
        copy.wait_recv()
    moved = to_plane(14, pages_ref, fetched)
    eye = lax.broadcasted_iota(jnp.int32, (HEAD, HEAD), 0) == lax.broadcasted_iota(
        jnp.int32, (HEAD, HEAD), 1
    )
    for h in range(2):
        for g in range(NY):
            levels = [lses[i, g, h, 0:1, :] for i in range(NX)]
            top = jnp.maximum(jnp.maximum(levels[0], levels[1]), jnp.maximum(levels[2], levels[3]))
            shares = [jnp.exp2(level - top) for level in levels]
            whole = shares[0] + shares[1] + shares[2] + shares[3]
            columns = [
                jnp.sum(jnp.where(eye, share / whole, 0.0), 1, keepdims=True) for share in shares
            ]
            for a in range(2):
                lanes = slice(a * HEAD, (a + 1) * HEAD)
                value = 0.0
                for i in range(NX):
                    value += columns[i][a * BLOCK : (a + 1) * BLOCK] * held[i, g, h, :, lanes].astype(F32)
                context[h, :, (2 * g + a) * HEAD : (2 * g + a + 1) * HEAD] = value.astype(BF16)
    trades = []
    theirs = context[partner]
    for n in range(CHUNKS):
        cols = slice(n * CHUNK, (n + 1) * CHUNK)
        outgoing[n] = jnp.dot(theirs, weights[:, cols], preferred_element_type=F32).astype(BF16)
        trades.append(send(21 + n, outgoing.at[n], incoming.at[n], (d, partner)))
    ours = context[r]
    for n in range(CHUNKS):
        cols = slice(n * CHUNK, (n + 1) * CHUNK)
        mine[:, cols] = tok[:, cols].astype(F32) + jnp.dot(
            ours, weights[:, cols], preferred_element_type=F32
        )
    for n in range(CHUNKS):
        cols = slice(n * CHUNK, (n + 1) * CHUNK)
        trades[n].wait_recv()
        out_ref[:, cols] = (mine[:, cols] + incoming[n].astype(F32)).astype(BF16)
    for copy in moved:
        copy.wait_recv()
    for j in range(SLOTS):
        at = column[j]
        held_here = jnp.full((2, PAGE, HEAD), at, jnp.int32) >= 0
        source = jnp.maximum(at, 0)
        for g in range(NY):
            page = fetched[source, g, j].astype(F32)
            cache_ref[j, :, :, g * HEAD : (g + 1) * HEAD] = jnp.where(held_here, page, 0.0).astype(BF16)
    for copy in parts + moved + trades:
        copy.wait_send()


def finish(column, o, lse, pages, w_out, tokens):
    count = 21 + CHUNKS
    return pl.pallas_call(
        finish_kernel,
        out_shape=(
            jax.ShapeDtypeStruct((BLOCK, WIDTH), BF16),
            jax.ShapeDtypeStruct((SLOTS, 2, PAGE, KCOLS), BF16),
        ),
        in_specs=[SMEM, ANY, ANY, ANY, HBM, HBM],
        out_specs=(VMEM, VMEM),
        scratch_shapes=[
            pltpu.VMEM((NX, NY, 2, BLOCK, 2 * HEAD), BF16),
            pltpu.VMEM((NX, NY, 2, 8, 2 * BLOCK), F32),
            pltpu.VMEM((NX, NY, SLOTS, 2, PAGE, HEAD), BF16),
            pltpu.VMEM((QCOLS, WIDTH), BF16),
            pltpu.VMEM((BLOCK, WIDTH), BF16),
            pltpu.VMEM((2, BLOCK, QCOLS), BF16),
            pltpu.VMEM((BLOCK, WIDTH), F32),
            pltpu.VMEM((CHUNKS, BLOCK, CHUNK), BF16),
            pltpu.VMEM((CHUNKS, BLOCK, CHUNK), BF16),
            pltpu.SemaphoreType.DMA((count,)),
            pltpu.SemaphoreType.DMA((count,)),
            pltpu.SemaphoreType.DMA((5,)),
        ],
        compiler_params=pltpu.CompilerParams(
            collective_id=2, has_side_effects=True, vmem_limit_bytes=32 * MIB
        ),
        name="finish",
    )(column, o, lse, pages, w_out, tokens)


def chosen(mask, values, axis):
    return jnp.sum(jnp.where(mask, values, 0), axis)


def tables(lengths, block_split, page_slot):
    d = lax.axis_index("seq")
    y, x, z, c = coords(d)
    iota = lambda n: jnp.arange(n, dtype=jnp.int32)
    four = iota(4)
    ends = chosen(four[None, :] <= four[:, None], lengths[None, :], 1)
    begins = ends - lengths

    def start_of(pos):
        return jnp.max(jnp.where(pos[:, None] >= begins[None, :], begins[None, :], 0), 1)

    own = block_split[d]
    pos = jnp.concatenate([own * BLOCK + iota(BLOCK), (2 * NSEQ - 1 - own) * BLOCK + iota(BLOCK)])
    rel = (pos - start_of(pos)).astype(F32)
    inv_freq = jnp.power(THETA, -(jnp.arange(HEAD // 2, dtype=F32) * (2.0 / HEAD)))
    angle = rel[:, None] * inv_freq[None, :]
    cosine, sine = jnp.cos(angle), jnp.sin(angle)
    cosine = jnp.concatenate([cosine, cosine], 1)
    sine = jnp.concatenate([-sine, sine], 1)
    grid = block_split.reshape(NY, NX, NZ, NC)
    line = lax.dynamic_index_in_dim(grid, x, 1, keepdims=False)
    line = jnp.transpose(line, (1, 2, 0)).reshape(32)
    blocks = jnp.stack([line, 2 * NSEQ - 1 - line], 1).reshape(64)
    rank = jnp.sum((blocks[None, :] < blocks[:, None]).astype(jnp.int32), 1)
    hit = rank[None, :] == iota(64)[:, None]
    order = chosen(hit, iota(64)[None, :], 1)
    sorted_blocks = chosen(hit, blocks[None, :], 1)
    beyond = jnp.full((STEP,), 1 << 14, jnp.int32)
    across = jnp.transpose(grid[:, :, z, c]).reshape(NXY)
    qblocks = jnp.stack([across, 2 * NSEQ - 1 - across], 1).reshape(2 * NXY)
    qrank = jnp.sum((qblocks[None, :] < qblocks[:, None]).astype(jnp.int32), 1)
    qhit = qrank[None, :] == iota(2 * NXY)[:, None]
    qorder = chosen(qhit, iota(2 * NXY)[None, :], 1)
    qsorted = chosen(qhit, qblocks[None, :], 1)
    qstart = start_of(qsorted * BLOCK) // BLOCK
    lo = jnp.sum((blocks[None, :] < qstart[:, None]).astype(jnp.int32), 1)
    hi = jnp.sum((blocks[None, :] <= qsorted[:, None]).astype(jnp.int32), 1)
    lo = jnp.min(lo.reshape(GROUPS, QUAD), 1) // 2 * 2
    hi = jnp.max(hi.reshape(GROUPS, QUAD), 1)
    steps = (hi - lo + STEP - 1) // STEP
    devices = index_of(iota(NY)[None, :], iota(NX)[:, None], z, c).reshape(NXY)
    slots = (devices[:, None] * SLOTS + iota(SLOTS)[None, :]).reshape(NXY * SLOTS)
    page = chosen(page_slot[None, :] == slots[:, None], iota(512)[None, :], 1)
    at = chosen(blocks[None, :] == (page // 2)[:, None], iota(64)[None, :], 1)
    sources = at * 2 + page % 2
    table = jnp.concatenate(
        [order, sorted_blocks, beyond, qorder, qsorted, lo, steps, begins, sources]
    )
    my_found = page_slot[None, :] == (d * SLOTS + iota(SLOTS))[:, None]
    my_page = chosen(my_found, iota(512)[None, :], 1)
    my_block = (my_page // 2)[:, None]
    holder = chosen(
        (block_split[None, :] == my_block) | (2 * NSEQ - 1 - block_split[None, :] == my_block),
        iota(NSEQ)[None, :],
        1,
    )
    column = jnp.where(jnp.any(my_found, 1), (holder // 16) % NX, -1)
    return cosine, sine, table, column


def on_device(
    tokens, norm_gain, w_query, key_projection, value_projection, w_out, lengths, block_split, page_slot
):
    cosine, sine, table, column = tables(lengths, block_split, page_slot)
    kvall, qall = gather(
        tokens, norm_gain.reshape(1, WIDTH), w_query, key_projection, value_projection, cosine, sine
    )
    o, lse, pages = attend(
        table, qall.reshape(NXY, 2, BLOCK, 2 * HEAD), kvall.reshape(32, 2, 4, PAGE, HEAD)
    )
    return finish(column, o, lse, pages, w_out, tokens)


def solution(mesh):
    in_specs = (
        P("seq", None),
        P(),
        P(None, "req"),
        P(None, "req"),
        P(None, "req"),
        P("req", None),
        P(),
        P(),
        P(),
    )
    out_specs = (P(("seq", "req"), None), P("seq", None, None, "req"))
    return jax.shard_map(
        on_device, mesh=mesh, in_specs=in_specs, out_specs=out_specs, check_vma=False
    )
```

```python
import math

import jax
import jax.numpy as jnp
import numpy as np
from jax import lax
from jax.experimental import pallas as pl
from jax.experimental.pallas import tpu as pltpu
from jax.sharding import PartitionSpec as P

MESH = pl.DeviceIdType.MESH
ANY = pl.BlockSpec(memory_space=pl.ANY)
HBM = pl.BlockSpec(memory_space=pltpu.HBM)
VMEM = pl.BlockSpec(memory_space=pltpu.VMEM)
SMEM = pl.BlockSpec(memory_space=pltpu.SMEM)

NY, NX, NZ, NC = 2, 4, 8, 2
NSEQ = NY * NX * NZ * NC
NXY = NX * NY
HEAD = 128
BLOCK = 64
ROWS = 128
PAGE = 32
SLOTS = 8
WIDTH = 2048
QCOLS = 512
KCOLS = 256
THETA = 1000000.0
EPS = 1e-05
FAR = -1e30
FLOOR = -1e29
SCALE2 = math.log2(math.e) / math.sqrt(HEAD)
MIB = 1 << 20
BF16 = jnp.bfloat16
F32 = jnp.float32

EXTRA = 16
KEYS = NC * NY * ROWS
LANES = NXY * 2 * ROWS
BEYOND = 1 << 14
CHUNK = 512
CHUNKS = WIDTH // CHUNK

FREQ = np.power(
    np.float32(THETA), -(np.arange(HEAD // 2, dtype=np.float32) * np.float32(2.0 / HEAD))
).astype(np.float32)
FREQ = np.concatenate([FREQ, FREQ])[None, :]


def coords(d):
    return d // 64, (d // 16) % NX, (d // 2) % NZ, d % 2


def index_of(y, x, z, c):
    return ((y * NX + x) * NZ + z) * NC + c


def plane(y, x, z, c):
    return [
        ((x + i) % NX, y if j == 0 else 1 - y, index_of(y if j == 0 else 1 - y, (x + i) % NX, z, c))
        for j in range(NY)
        for i in range(NX)
    ]


NODES = [(0, 0)]
for _k in (1, 2, 3):
    NODES += [(1, -_k), (1, _k), (0, -_k), (0, _k)]
NODES += [(1, 4), (0, 4)]


def passed_on(own, dz):
    out = []
    if -3 < dz <= 0 or (dz == -3 and own):
        out.append(("up", dz - 1))
    if 0 <= dz < 3 or (dz == 3 and not own):
        out.append(("down", dz + 1))
    return [(to, 4 if abs(to_dz) == 4 else to_dz) for to, to_dz in out]


def prompt_start(pos, begins):
    first = jnp.zeros_like(pos)
    for begin in begins:
        first = jnp.where(pos >= begin, begin, first)
    return first


def begins_of(lengths):
    one = lengths[0]
    two = one + lengths[1]
    return one, two, two + lengths[2]


def rotation(own, begins, freq):
    row = lax.broadcasted_iota(jnp.int32, (ROWS, HEAD), 0)
    pos = jnp.where(
        row < BLOCK, own * BLOCK + row, (2 * NSEQ - 1 - own) * BLOCK + row - BLOCK
    )
    angle = (pos - prompt_start(pos, begins)).astype(F32) * freq
    turns = jnp.floor(angle * (2.0 / math.pi) + 0.5)
    rest = angle - turns * 1.5703125
    rest = rest - turns * 4.837512969970703125e-4
    rest = rest - turns * 7.54978995489188216e-8
    quarter = turns.astype(jnp.int32) & 3
    sq = rest * rest
    sine = rest + rest * sq * (-1.6666654611e-1 + sq * (8.3321608736e-3 - sq * 1.9515295891e-4))
    cosine = (
        1.0
        - 0.5 * sq
        + sq * sq * (4.166664568298827e-2 + sq * (-1.388731625493765e-3 + sq * 2.443315711809948e-5))
    )
    odd = (quarter & 1) == 1
    turned_sine = jnp.where(odd, cosine, sine)
    turned_cosine = jnp.where(odd, sine, cosine)
    lower = lax.broadcasted_iota(jnp.int32, (ROWS, HEAD), 1) < HEAD // 2
    minus = (quarter >= 2) != lower
    sine = jnp.where(minus, -turned_sine, turned_sine)
    cosine = jnp.where((quarter == 1) | (quarter == 2), -turned_cosine, turned_cosine)
    return cosine, sine


def diagonal():
    return lax.broadcasted_iota(jnp.int32, (HEAD, HEAD), 0) == lax.broadcasted_iota(
        jnp.int32, (HEAD, HEAD), 1
    )


def stand(row, eye):
    return jnp.sum(jnp.where(eye, jnp.broadcast_to(row, (HEAD, HEAD)), 0.0), 1, keepdims=True)


def table_kernel(split_ref, slot_ref, table_ref):
    y, x, z, c = coords(lax.axis_index("seq"))
    eye = diagonal()
    sub = lax.broadcasted_iota(jnp.int32, (HEAD, HEAD), 0)
    row_lane = lax.broadcasted_iota(jnp.int32, (1, HEAD), 1)

    def pick(mask, value):
        return jnp.sum(jnp.where(mask, value, 0.0), 0, keepdims=True)

    ys, xs, zs, cs = coords(sub)
    split_col = jnp.broadcast_to(stand(split_ref[...].astype(F32), eye), (HEAD, HEAD))
    halves = (split_col, 2 * NSEQ - 1 - split_col)
    place = row_lane // SLOTS % NXY
    wanted = index_of(place % NY, place // NY, z, c) * SLOTS + row_lane % SLOTS
    page, found = 0.0, 0.0
    for k in range(4):
        slots = jnp.broadcast_to(stand(slot_ref[k : k + 1, :].astype(F32), eye), (HEAD, HEAD))
        hit = slots == wanted.astype(F32)
        page += pick(hit, (sub + HEAD * k).astype(F32))
        found += pick(hit, 1.0)
    page = page.astype(jnp.int32)
    block = (page // 2).astype(F32)
    at, column = 0.0, 0.0
    for h in range(2):
        hit = halves[h] == block
        at += pick(hit & (xs == x), (2 * ((zs * NC + cs) * NY + ys) + h).astype(F32))
        column += pick(hit, xs.astype(F32))
    table_ref[0:1, :] = at.astype(jnp.int32) * 2 + page % 2
    table_ref[1:2, :] = jnp.where(found > 0.5, column, -1.0).astype(jnp.int32)
    table_ref[2:, :] = jnp.zeros((6, HEAD), jnp.int32)


def make_table(block_split, page_slot):
    return pl.pallas_call(
        table_kernel,
        out_shape=jax.ShapeDtypeStruct((8, HEAD), jnp.int32),
        in_specs=[VMEM, VMEM],
        out_specs=VMEM,
        name="table",
    )(block_split.reshape(1, NSEQ), page_slot.reshape(4, HEAD))


NODES = [(0, 0)]
for _k in (1, 2, 3):
    NODES += [(1, -_k), (1, _k), (0, -_k), (0, _k)]
NODES += [(1, 4), (0, 4)]
PLACES = [(own, dz) for own in (1, 0) for dz in (0, -1, 1, -2, 2, -3, 3, 4)]


def passed_on(own, dz):
    out = []
    if -3 < dz <= 0 or (dz == -3 and own):
        out.append(("up", dz - 1))
    if 0 <= dz < 3 or (dz == 3 and not own):
        out.append(("down", dz + 1))
    return [(to, 4 if abs(to_dz) == 4 else to_dz) for to, to_dz in out]


def layer_kernel(
    lengths, split, table, tok_hbm, gain_ref, wq_hbm, wk_hbm, wv_hbm, wo_hbm, freq_ref,
    out_ref, cache_ref,
    tok, wq, wk, wv, wo, normed, proj, kv, q, kvall, qall, turned, acc, top,
    parts, levels, held, lses, pages, fetched, context, mine, outgoing, incoming,
    load_sem, send_sem, recv_sem,
):
    d, r = lax.axis_index("seq"), lax.axis_index("req")
    y, x, z, c = coords(d)
    partner = 1 - r
    loads = [pltpu.make_async_copy(tok_hbm, tok, load_sem.at[0])]
    for k in range(4):
        rows = pl.ds(512 * k, 512)
        for n, (src, dst) in enumerate(((wq_hbm, wq), (wk_hbm, wk), (wv_hbm, wv))):
            loads.append(
                pltpu.make_async_copy(src.at[rows], dst.at[rows], load_sem.at[1 + 3 * k + n])
            )
    load_wo = pltpu.make_async_copy(wo_hbm, wo, load_sem.at[13])
    for copy in loads + [load_wo]:
        copy.start()
    near = {
        "sib": (index_of(y, x, z, 1 - c), r),
        "up": (index_of(y, x, (z + 1) % NZ, c), r),
        "down": (index_of(y, x, (z + NZ - 1) % NZ, c), r),
        "req": (d, partner),
    }
    peers = plane(y, x, z, c)
    barrier = pltpu.get_barrier_semaphore()
    everyone = list(near.values()) + [(peer[2], r) for peer in peers[1:]]
    for peer in everyone:
        pl.semaphore_signal(barrier, inc=1, device_id=peer, device_id_type=MESH)

    copies = {}

    def plan(name, src, dst, to):
        n = len(copies)
        copies[name] = pltpu.make_async_remote_copy(
            src_ref=src,
            dst_ref=dst,
            send_sem=send_sem.at[n],
            recv_sem=recv_sem.at[n],
            device_id=to,
            device_id_type=MESH,
        )

    def shard(own, dz):
        return kvall.at[(z + dz + NZ) % NZ, c, y if own else 1 - y]

    plan((0, 0), kv.at[1 - y], shard(1, 0), (peers[NX][2], r))
    for own, dz in PLACES:
        for to, far in passed_on(own, dz):
            plan((own, far), shard(own, dz), shard(own, dz), near[to])
        plan(("s", own, dz), shard(own, dz), shard(own, dz), near["sib"])
    for n, (px, py, peer) in enumerate(peers):
        if n:
            to = (peer, r)
            plan(("q", n), q.at[py], qall.at[x, y], to)
            plan(("l", n), levels.at[px * NY + py], lses.at[x, y], to)
            plan(("o", n), parts.at[px * NY + py], held.at[x, y], to)
            plan(("p", n), pages.at[px * NY + py], fetched.at[x, y], to)
    for n in range(CHUNKS):
        plan(("t", n), outgoing.at[n], incoming.at[n], near["req"])
    others = range(1, NXY)

    def relay(*nodes):
        for own, dz in nodes:
            if (own, dz) != (1, 0):
                copies[own, dz].wait_recv()
            for _, far in passed_on(own, dz):
                copies[own, far].start()
            copies["s", own, dz].start()

    begins = begins_of(lengths)
    cosine, sine = rotation(split[d], begins, freq_ref[...])
    loads[0].wait()
    wide = tok[...].astype(F32)
    inv = lax.rsqrt(jnp.mean(wide * wide, -1, keepdims=True) + EPS)
    normed[...] = (wide * inv * gain_ref[...]).astype(BF16)
    for k in range(4):
        for copy in loads[1 + 3 * k : 4 + 3 * k]:
            copy.wait()
        rows = slice(512 * k, 512 * (k + 1))
        part = normed[:, rows]
        for cols, weights in ((slice(0, 512), wq), (slice(512, 768), wk), (slice(768, 1024), wv)):
            value = jnp.dot(part, weights[rows, :], preferred_element_type=F32)
            if k == 0:
                proj[:, cols] = value
            else:
                proj[:, cols] += value
    for h in range(6):
        u = proj[:, HEAD * h : HEAD * (h + 1)]
        rotated = (u * cosine + pltpu.roll(u, HEAD // 2, 1) * sine).astype(BF16)
        if h < 4:
            q[h // 2, h % 2] = rotated
        else:
            kv[h - 4, 0] = rotated.reshape(4, PAGE, HEAD)
    for g in range(2):
        kv[g, 1] = proj[:, 768 + HEAD * g : 768 + HEAD * (g + 1)].astype(BF16).reshape(4, PAGE, HEAD)
    kvall[z, c, y] = kv[y]
    qall[x, y] = q[y]
    pl.semaphore_wait(barrier, len(everyone))
    relay((1, 0))
    copies[0, 0].start()
    for n in others:
        copies["q", n].start()

    lane = lax.broadcasted_iota(jnp.int32, (1, ROWS), 1)
    pos = []
    for px in range(NX):
        for py in range(NY):
            block = split[index_of(py, px, z, c)]
            row = jnp.where(
                lane < BLOCK, block * BLOCK + lane, (2 * NSEQ - 1 - block) * BLOCK + lane - BLOCK
            )
            pos += [row, row]
    pos = jnp.concatenate(pos, 1)
    first = prompt_start(pos, begins)
    turned[HEAD:, :] = jnp.ones((EXTRA, KEYS), BF16)
    top[...] = jnp.full_like(top, FLOOR)
    acc[...] = jnp.zeros_like(acc)
    inner = lax.broadcasted_iota(jnp.int32, (BLOCK, LANES), 0)

    def build_pages():
        def one(n, _):
            at = table[0, n]
            for part in range(2):
                pages[n // SLOTS, n % SLOTS, part] = kvall[
                    at // 16, at // 8 % 2, at // 4 % 2, part, at % 4
                ]
            return 0

        lax.fori_loop(0, NXY * SLOTS, one, 0)

    def sibling(*places):
        for own, dz in places:
            copies["s", own, dz].wait_recv()

    def batch(i, _):
        @pl.when(i == 0)
        def _():
            relay((0, 0), (1, -1), (1, 1))
            relay((1, -2), (1, 2), (0, -1), (0, 1))
            sibling((1, 0), (0, 0))
            for n in others:
                copies["q", n].wait_recv()

        @pl.when(i == 1)
        def _():
            sibling((1, -1), (0, -1))

        @pl.when(i == 2)
        def _():
            relay((1, -3), (1, 3), (0, -2), (0, 2))
            sibling((1, 1), (0, 1))

        @pl.when(i == 3)
        def _():
            sibling((1, -2), (0, -2))

        @pl.when(i == 4)
        def _():
            relay((1, 4), (0, -3), (0, 3))
            sibling((1, 2), (0, 2))

        @pl.when(i == 5)
        def _():
            sibling((1, -3), (0, -3))

        @pl.when(i == 6)
        def _():
            relay((0, 4))
            sibling((1, 3), (0, 3))

        @pl.when(i == 7)
        def _():
            sibling((1, 4), (0, 4))
            build_pages()
            for n in range(1, NX):
                copies["p", n].start()

        half = (i + 1) // 2
        far = (z + NZ + half * (1 - i % 2 * 2)) % NZ
        pieces = [(cc, yy) for cc in range(NC) for yy in range(NY)]
        for n, (cc, yy) in enumerate(pieces):
            turned[:HEAD, n * ROWS : (n + 1) * ROWS] = jnp.transpose(
                kvall[far, cc, yy, 1].reshape(ROWS, HEAD)
            )
        keys = jnp.concatenate([kvall[far, cc, yy, 0].reshape(ROWS, HEAD) for cc, yy in pieces], 0)
        queries = qall[...].reshape(LANES, HEAD)
        s = lax.dot_general(keys, queries, (((1,), (1,)), ((), ())), preferred_element_type=F32)
        masked = []
        for n, (cc, yy) in enumerate(pieces):
            block = split[index_of(yy, x, far, cc)]
            for h in range(2):
                base = (block if h == 0 else 2 * NSEQ - 1 - block) * BLOCK
                visible = (inner >= first - base) & (inner <= pos - base)
                at = n * ROWS + h * BLOCK
                masked.append(jnp.where(visible, s[at : at + BLOCK], FAR))
        s = jnp.concatenate(masked, 0)
        before = top[...]
        higher = jnp.maximum(before, jnp.max(s, 0, keepdims=True))
        e = jnp.exp2((s - higher) * SCALE2).astype(BF16)
        fade = jnp.exp2((before - higher) * SCALE2)
        top[...] = higher
        acc[...] = acc[...] * fade + jnp.dot(turned[...], e, preferred_element_type=F32)
        return 0

    lax.fori_loop(0, NZ, batch, 0)

    total = acc[HEAD : HEAD + 1, :]
    seen = total > 0.0
    safe = jnp.where(seen, total, 1.0)
    lse = jnp.where(seen, top[...] * SCALE2 + jnp.log2(safe), FAR)
    inverse = 1.0 / safe
    for n in range(NXY):
        cols = slice(n * 2 * ROWS, (n + 1) * 2 * ROWS)
        parts[n] = (acc[:HEAD, cols] * inverse[:, cols]).astype(BF16)
        levels[n] = jnp.broadcast_to(lse[:, cols], (8, 2 * ROWS))
    for n in others:
        copies["l", n].start()
        copies["o", n].start()
    held[x, y] = parts[x * NY + y]
    lses[x, y] = levels[x * NY + y]
    fetched[x, y] = pages[x * NY + y]
    load_wo.wait()
    for n in others:
        copies["l", n].wait_send()
        copies["o", n].wait_send()
    for n in range(NX, NXY):
        copies["p", n].start()
    for n in others:
        copies["l", n].wait_recv()
        copies["o", n].wait_recv()
    for g in range(NY):
        rows = [lses[i, g, 0:1, :] for i in range(NX)]
        peak = jnp.maximum(jnp.maximum(rows[0], rows[1]), jnp.maximum(rows[2], rows[3]))
        shares = [jnp.exp2(row - peak) for row in rows]
        whole = shares[0] + shares[1] + shares[2] + shares[3]
        value = 0.0
        for i in range(NX):
            value += held[i, g].astype(F32) * (shares[i] / whole)
        for a in range(2):
            cols = slice((2 * g + a) * HEAD, (2 * g + a + 1) * HEAD)
            rows = jnp.transpose(value[:, a * ROWS : (a + 1) * ROWS].astype(BF16))
            context[0, :, cols] = rows[:BLOCK]
            context[1, :, cols] = rows[BLOCK:]

    theirs = context[partner]
    for n in range(CHUNKS):
        cols = slice(n * CHUNK, (n + 1) * CHUNK)
        outgoing[n] = jnp.dot(theirs, wo[:, cols], preferred_element_type=F32).astype(BF16)
        copies["t", n].start()
    ours = context[r]
    residual = tok[pl.ds(pl.multiple_of(r * BLOCK, BLOCK), BLOCK), :]
    for n in range(CHUNKS):
        cols = slice(n * CHUNK, (n + 1) * CHUNK)
        mine[:, cols] = residual[:, cols].astype(F32) + jnp.dot(
            ours, wo[:, cols], preferred_element_type=F32
        )
    for n in range(CHUNKS):
        cols = slice(n * CHUNK, (n + 1) * CHUNK)
        copies["t", n].wait_recv()
        out_ref[:, cols] = (mine[:, cols] + incoming[n].astype(F32)).astype(BF16)
    for n in others:
        copies["p", n].wait_recv()
    for j in range(SLOTS):
        at = table[1, (x * NY + y) * SLOTS + j]
        here = jnp.full((2, PAGE, HEAD), at, jnp.int32) >= 0
        source = jnp.maximum(at, 0)
        for g in range(NY):
            page = fetched[source, g, j].astype(F32)
            cache_ref[j, :, :, g * HEAD : (g + 1) * HEAD] = jnp.where(here, page, 0.0).astype(BF16)
    for name, copy in copies.items():
        if name[0] not in ("l", "o"):
            copy.wait_send()


COPIES = 15 + 16 + 4 * (NXY - 1) + CHUNKS


def on_device(
    tokens, norm_gain, w_query, key_projection, value_projection, w_out, lengths, block_split, page_slot
):
    return pl.pallas_call(
        layer_kernel,
        out_shape=(
            jax.ShapeDtypeStruct((BLOCK, WIDTH), BF16),
            jax.ShapeDtypeStruct((SLOTS, 2, PAGE, KCOLS), BF16),
        ),
        in_specs=[SMEM, SMEM, SMEM, HBM, VMEM, HBM, HBM, HBM, HBM, VMEM],
        out_specs=(VMEM, VMEM),
        scratch_shapes=[
            pltpu.VMEM((ROWS, WIDTH), BF16),
            pltpu.VMEM((WIDTH, QCOLS), BF16),
            pltpu.VMEM((WIDTH, KCOLS), BF16),
            pltpu.VMEM((WIDTH, KCOLS), BF16),
            pltpu.VMEM((QCOLS, WIDTH), BF16),
            pltpu.VMEM((ROWS, WIDTH), BF16),
            pltpu.VMEM((ROWS, 1024), F32),
            pltpu.VMEM((2, 2, 4, PAGE, HEAD), BF16),
            pltpu.VMEM((2, 2, ROWS, HEAD), BF16),
            pltpu.VMEM((NZ, NC, NY, 2, 4, PAGE, HEAD), BF16),
            pltpu.VMEM((NX, NY, 2, ROWS, HEAD), BF16),
            pltpu.VMEM((HEAD + EXTRA, KEYS), BF16),
            pltpu.VMEM((HEAD + EXTRA, LANES), F32),
            pltpu.VMEM((1, LANES), F32),
            pltpu.VMEM((NXY, HEAD, 2 * ROWS), BF16),
            pltpu.VMEM((NXY, 8, 2 * ROWS), F32),
            pltpu.VMEM((NX, NY, HEAD, 2 * ROWS), BF16),
            pltpu.VMEM((NX, NY, 8, 2 * ROWS), F32),
            pltpu.VMEM((NXY, SLOTS, 2, PAGE, HEAD), BF16),
            pltpu.VMEM((NX, NY, SLOTS, 2, PAGE, HEAD), BF16),
            pltpu.VMEM((2, BLOCK, QCOLS), BF16),
            pltpu.VMEM((BLOCK, WIDTH), F32),
            pltpu.VMEM((CHUNKS, BLOCK, CHUNK), BF16),
            pltpu.VMEM((CHUNKS, BLOCK, CHUNK), BF16),
            pltpu.SemaphoreType.DMA((14,)),
            pltpu.SemaphoreType.DMA((COPIES,)),
            pltpu.SemaphoreType.DMA((COPIES,)),
        ],
        compiler_params=pltpu.CompilerParams(
            collective_id=1, has_side_effects=True, vmem_limit_bytes=60 * MIB
        ),
        name="layer",
    )(
        lengths, block_split, make_table(block_split, page_slot), tokens, norm_gain.reshape(1, WIDTH), w_query,
        key_projection, value_projection, w_out, jnp.asarray(FREQ),
    )


def solution(mesh):
    in_specs = (
        P("seq", None),
        P(),
        P(None, "req"),
        P(None, "req"),
        P(None, "req"),
        P("req", None),
        P(),
        P(),
        P(),
    )
    out_specs = (P(("seq", "req"), None), P("seq", None, None, "req"))
    return jax.shard_map(
        on_device, mesh=mesh, in_specs=in_specs, out_specs=out_specs, check_vma=False
    )
```

```python
import math

import jax
import jax.numpy as jnp
import numpy as np
from jax import lax
from jax.experimental import pallas as pl
from jax.experimental.pallas import tpu as pltpu
from jax.sharding import PartitionSpec as P

MESH = pl.DeviceIdType.MESH
ANY = pl.BlockSpec(memory_space=pl.ANY)
HBM = pl.BlockSpec(memory_space=pltpu.HBM)
VMEM = pl.BlockSpec(memory_space=pltpu.VMEM)
SMEM = pl.BlockSpec(memory_space=pltpu.SMEM)

NY, NX, NZ, NC = 2, 4, 8, 2
NSEQ = NY * NX * NZ * NC
NXY = NX * NY
HEAD = 128
BLOCK = 64
ROWS = 128
PAGE = 32
SLOTS = 8
WIDTH = 2048
QCOLS = 512
KCOLS = 256
THETA = 1000000.0
EPS = 1e-05
FAR = -1e30
FLOOR = -1e29
SCALE2 = math.log2(math.e) / math.sqrt(HEAD)
MIB = 1 << 20
BF16 = jnp.bfloat16
F32 = jnp.float32

EXTRA = 16
KEYS = NC * NY * ROWS
LANES = NXY * 2 * ROWS
BEYOND = 1 << 14
CHUNK = 512
CHUNKS = WIDTH // CHUNK

FREQ = np.power(
    np.float32(THETA), -(np.arange(HEAD // 2, dtype=np.float32) * np.float32(2.0 / HEAD))
).astype(np.float32)
FREQ = np.concatenate([FREQ, FREQ])[None, :]


def coords(d):
    return d // 64, (d // 16) % NX, (d // 2) % NZ, d % 2


def index_of(y, x, z, c):
    return ((y * NX + x) * NZ + z) * NC + c


def plane(y, x, z, c):
    return [
        ((x + i) % NX, y if j == 0 else 1 - y, index_of(y if j == 0 else 1 - y, (x + i) % NX, z, c))
        for j in range(NY)
        for i in range(NX)
    ]


NODES = [(0, 0)]
for _k in (1, 2, 3):
    NODES += [(1, -_k), (1, _k), (0, -_k), (0, _k)]
NODES += [(1, 4), (0, 4)]


def passed_on(own, dz):
    out = []
    if -3 < dz <= 0 or (dz == -3 and own):
        out.append(("up", dz - 1))
    if 0 <= dz < 3 or (dz == 3 and not own):
        out.append(("down", dz + 1))
    return [(to, 4 if abs(to_dz) == 4 else to_dz) for to, to_dz in out]


def prompt_start(pos, begins):
    first = jnp.zeros_like(pos)
    for begin in begins:
        first = jnp.where(pos >= begin, begin, first)
    return first


def begins_of(lengths):
    one = lengths[0]
    two = one + lengths[1]
    return one, two, two + lengths[2]


def rotation(own, begins, freq):
    row = lax.broadcasted_iota(jnp.int32, (ROWS, HEAD), 0)
    pos = jnp.where(
        row < BLOCK, own * BLOCK + row, (2 * NSEQ - 1 - own) * BLOCK + row - BLOCK
    )
    angle = (pos - prompt_start(pos, begins)).astype(F32) * freq
    turns = jnp.floor(angle * (2.0 / math.pi) + 0.5)
    rest = angle - turns * 1.5703125
    rest = rest - turns * 4.837512969970703125e-4
    rest = rest - turns * 7.54978995489188216e-8
    quarter = turns.astype(jnp.int32) & 3
    sq = rest * rest
    sine = rest + rest * sq * (-1.6666654611e-1 + sq * (8.3321608736e-3 - sq * 1.9515295891e-4))
    cosine = (
        1.0
        - 0.5 * sq
        + sq * sq * (4.166664568298827e-2 + sq * (-1.388731625493765e-3 + sq * 2.443315711809948e-5))
    )
    odd = (quarter & 1) == 1
    turned_sine = jnp.where(odd, cosine, sine)
    turned_cosine = jnp.where(odd, sine, cosine)
    lower = lax.broadcasted_iota(jnp.int32, (ROWS, HEAD), 1) < HEAD // 2
    minus = (quarter >= 2) != lower
    sine = jnp.where(minus, -turned_sine, turned_sine)
    cosine = jnp.where((quarter == 1) | (quarter == 2), -turned_cosine, turned_cosine)
    return cosine, sine


def diagonal():
    return lax.broadcasted_iota(jnp.int32, (HEAD, HEAD), 0) == lax.broadcasted_iota(
        jnp.int32, (HEAD, HEAD), 1
    )


def stand(row, eye):
    return jnp.sum(jnp.where(eye, jnp.broadcast_to(row, (HEAD, HEAD)), 0.0), 1, keepdims=True)


def table_kernel(split_ref, slot_ref, table_ref):
    y, x, z, c = coords(lax.axis_index("seq"))
    eye = diagonal()
    sub = lax.broadcasted_iota(jnp.int32, (HEAD, HEAD), 0)
    row_lane = lax.broadcasted_iota(jnp.int32, (1, HEAD), 1)

    def pick(mask, value):
        return jnp.sum(jnp.where(mask, value, 0.0), 0, keepdims=True)

    ys, xs, zs, cs = coords(sub)
    split_col = jnp.broadcast_to(stand(split_ref[...].astype(F32), eye), (HEAD, HEAD))
    halves = (split_col, 2 * NSEQ - 1 - split_col)
    place = row_lane // SLOTS % NXY
    wanted = index_of(place % NY, place // NY, z, c) * SLOTS + row_lane % SLOTS
    page, found = 0.0, 0.0
    for k in range(4):
        slots = jnp.broadcast_to(stand(slot_ref[k : k + 1, :].astype(F32), eye), (HEAD, HEAD))
        hit = slots == wanted.astype(F32)
        page += pick(hit, (sub + HEAD * k).astype(F32))
        found += pick(hit, 1.0)
    page = page.astype(jnp.int32)
    block = (page // 2).astype(F32)
    at, column = 0.0, 0.0
    for h in range(2):
        hit = halves[h] == block
        at += pick(hit & (xs == x), (2 * ((zs * NC + cs) * NY + ys) + h).astype(F32))
        column += pick(hit, xs.astype(F32))
    table_ref[0:1, :] = at.astype(jnp.int32) * 2 + page % 2
    table_ref[1:2, :] = jnp.where(found > 0.5, column, -1.0).astype(jnp.int32)
    table_ref[2:, :] = jnp.zeros((6, HEAD), jnp.int32)


def make_table(block_split, page_slot):
    return pl.pallas_call(
        table_kernel,
        out_shape=jax.ShapeDtypeStruct((8, HEAD), jnp.int32),
        in_specs=[VMEM, VMEM],
        out_specs=VMEM,
        name="table",
    )(block_split.reshape(1, NSEQ), page_slot.reshape(4, HEAD))


NODES = [(0, 0)]
for _k in (1, 2, 3):
    NODES += [(1, -_k), (1, _k), (0, -_k), (0, _k)]
NODES += [(1, 4), (0, 4)]
PLACES = [(own, dz) for own in (1, 0) for dz in (0, -1, 1, -2, 2, -3, 3, 4)]


def passed_on(own, dz):
    out = []
    if -3 < dz <= 0 or (dz == -3 and own):
        out.append(("up", dz - 1))
    if 0 <= dz < 3 or (dz == 3 and not own):
        out.append(("down", dz + 1))
    return [(to, 4 if abs(to_dz) == 4 else to_dz) for to, to_dz in out]


def layer_kernel(
    lengths, split, table, tok_hbm, gain_ref, wq_hbm, wk_hbm, wv_hbm, wo_hbm, freq_ref,
    out_ref, cache_ref,
    tok, wq, wk, wv, wo, normed, proj, kv, q, kvall, qall, turned, acc, top,
    parts, levels, held, lses, pages, fetched, swapped, swapping, context, mine, outgoing, incoming,
    load_sem, send_sem, recv_sem,
):
    d, r = lax.axis_index("seq"), lax.axis_index("req")
    y, x, z, c = coords(d)
    partner = 1 - r
    loads = [pltpu.make_async_copy(tok_hbm, tok, load_sem.at[0])]
    for k in range(4):
        rows = pl.ds(512 * k, 512)
        for n, (src, dst) in enumerate(((wq_hbm, wq), (wk_hbm, wk), (wv_hbm, wv))):
            loads.append(
                pltpu.make_async_copy(src.at[rows], dst.at[rows], load_sem.at[1 + 3 * k + n])
            )
    load_wo = pltpu.make_async_copy(wo_hbm, wo, load_sem.at[13])
    for copy in loads + [load_wo]:
        copy.start()
    near = {
        "sib": (index_of(y, x, z, 1 - c), r),
        "up": (index_of(y, x, (z + 1) % NZ, c), r),
        "down": (index_of(y, x, (z + NZ - 1) % NZ, c), r),
        "req": (d, partner),
    }
    peers = plane(y, x, z, c)
    barrier = pltpu.get_barrier_semaphore()
    everyone = list(near.values()) + [(peer[2], r) for peer in peers[1:]]
    for peer in everyone:
        pl.semaphore_signal(barrier, inc=1, device_id=peer, device_id_type=MESH)

    copies = {}

    def plan(name, src, dst, to):
        n = len(copies)
        copies[name] = pltpu.make_async_remote_copy(
            src_ref=src,
            dst_ref=dst,
            send_sem=send_sem.at[n],
            recv_sem=recv_sem.at[n],
            device_id=to,
            device_id_type=MESH,
        )

    def shard(own, dz):
        return kvall.at[(z + dz + NZ) % NZ, c, y if own else 1 - y]

    plan((0, 0), kv.at[1 - y], shard(1, 0), (peers[NX][2], r))
    for own, dz in PLACES:
        for to, far in passed_on(own, dz):
            plan((own, far), shard(own, dz), shard(own, dz), near[to])
        plan(("s", own, dz), shard(own, dz), shard(own, dz), near["sib"])
    for n, (px, py, peer) in enumerate(peers):
        if n:
            to = (peer, r)
            plan(("q", n), q.at[py], qall.at[x, y], to)
            plan(("l", n), levels.at[px * NY + py], lses.at[x, y], to)
            plan(("o", n), parts.at[px * NY + py], held.at[x, y], to)
            if n < NX:
                plan(("p", n), pages.at[pl.ds(px * NY, NY)], fetched.at[x], to)
    for n in range(CHUNKS):
        plan(("t", n), outgoing.at[n], incoming.at[n], near["req"])
    plan(("w", 0), swapped, swapping, (peers[NX][2], r))
    others = range(1, NXY)

    def relay(*nodes):
        for own, dz in nodes:
            if (own, dz) != (1, 0):
                copies[own, dz].wait_recv()
            for _, far in passed_on(own, dz):
                copies[own, far].start()
            copies["s", own, dz].start()

    begins = begins_of(lengths)
    cosine, sine = rotation(split[d], begins, freq_ref[...])
    loads[0].wait()
    wide = tok[...].astype(F32)
    inv = lax.rsqrt(jnp.mean(wide * wide, -1, keepdims=True) + EPS)
    normed[...] = (wide * inv * gain_ref[...]).astype(BF16)
    for k in range(4):
        for copy in loads[1 + 3 * k : 4 + 3 * k]:
            copy.wait()
        rows = slice(512 * k, 512 * (k + 1))
        part = normed[:, rows]
        for cols, weights in ((slice(0, 512), wq), (slice(512, 768), wk), (slice(768, 1024), wv)):
            value = jnp.dot(part, weights[rows, :], preferred_element_type=F32)
            if k == 0:
                proj[:, cols] = value
            else:
                proj[:, cols] += value
    for h in range(6):
        u = proj[:, HEAD * h : HEAD * (h + 1)]
        rotated = (u * cosine + pltpu.roll(u, HEAD // 2, 1) * sine).astype(BF16)
        if h < 4:
            q[h // 2, h % 2] = rotated
        else:
            kv[h - 4, 0] = rotated.reshape(4, PAGE, HEAD)
    for g in range(2):
        kv[g, 1] = proj[:, 768 + HEAD * g : 768 + HEAD * (g + 1)].astype(BF16).reshape(4, PAGE, HEAD)
    kvall[z, c, y] = kv[y]
    qall[x, y] = q[y]
    pl.semaphore_wait(barrier, len(everyone))
    relay((1, 0))
    copies[0, 0].start()
    for n in others:
        copies["q", n].start()

    lane = lax.broadcasted_iota(jnp.int32, (1, ROWS), 1)
    pos = []
    for px in range(NX):
        for py in range(NY):
            block = split[index_of(py, px, z, c)]
            row = jnp.where(
                lane < BLOCK, block * BLOCK + lane, (2 * NSEQ - 1 - block) * BLOCK + lane - BLOCK
            )
            pos += [row, row]
    pos = jnp.concatenate(pos, 1)
    first = prompt_start(pos, begins)
    turned[HEAD:, :] = jnp.ones((EXTRA, KEYS), BF16)
    top[...] = jnp.full_like(top, FLOOR)
    acc[...] = jnp.zeros_like(acc)
    inner = lax.broadcasted_iota(jnp.int32, (BLOCK, LANES), 0)

    def build_pages():
        def one(n, _):
            at = table[0, n]
            for part in range(2):
                pages[n // SLOTS, n % SLOTS, part] = kvall[
                    at // 16, at // 8 % 2, at // 4 % 2, part, at % 4
                ]
            return 0

        lax.fori_loop(0, NXY * SLOTS, one, 0)

    def sibling(*places):
        for own, dz in places:
            copies["s", own, dz].wait_recv()

    def batch(i, _):
        @pl.when(i == 0)
        def _():
            relay((0, 0), (1, -1), (1, 1))
            relay((1, -2), (1, 2), (0, -1), (0, 1))
            sibling((1, 0), (0, 0))
            for n in others:
                copies["q", n].wait_recv()

        @pl.when(i == 1)
        def _():
            sibling((1, -1), (0, -1))

        @pl.when(i == 2)
        def _():
            relay((1, -3), (1, 3), (0, -2), (0, 2))
            sibling((1, 1), (0, 1))

        @pl.when(i == 3)
        def _():
            sibling((1, -2), (0, -2))

        @pl.when(i == 4)
        def _():
            relay((1, 4), (0, -3), (0, 3))
            sibling((1, 2), (0, 2))

        @pl.when(i == 5)
        def _():
            sibling((1, -3), (0, -3))

        @pl.when(i == 6)
        def _():
            relay((0, 4))
            sibling((1, 3), (0, 3))

        @pl.when(i == 7)
        def _():
            sibling((1, 4), (0, 4))
            build_pages()
            copies["p", 1].start()
            copies["p", 3].start()

        half = (i + 1) // 2
        far = (z + NZ + half * (1 - i % 2 * 2)) % NZ
        pieces = [(cc, yy) for cc in range(NC) for yy in range(NY)]
        for n, (cc, yy) in enumerate(pieces):
            turned[:HEAD, n * ROWS : (n + 1) * ROWS] = jnp.transpose(
                kvall[far, cc, yy, 1].reshape(ROWS, HEAD)
            )
        keys = jnp.concatenate([kvall[far, cc, yy, 0].reshape(ROWS, HEAD) for cc, yy in pieces], 0)
        queries = qall[...].reshape(LANES, HEAD)
        s = lax.dot_general(keys, queries, (((1,), (1,)), ((), ())), preferred_element_type=F32)
        masked = []
        for n, (cc, yy) in enumerate(pieces):
            block = split[index_of(yy, x, far, cc)]
            for h in range(2):
                base = (block if h == 0 else 2 * NSEQ - 1 - block) * BLOCK
                visible = (inner >= first - base) & (inner <= pos - base)
                at = n * ROWS + h * BLOCK
                masked.append(jnp.where(visible, s[at : at + BLOCK], FAR))
        s = jnp.concatenate(masked, 0)
        before = top[...]
        higher = jnp.maximum(before, jnp.max(s, 0, keepdims=True))
        e = jnp.exp2((s - higher) * SCALE2).astype(BF16)
        fade = jnp.exp2((before - higher) * SCALE2)
        top[...] = higher
        acc[...] = acc[...] * fade + jnp.dot(turned[...], e, preferred_element_type=F32)
        return 0

    lax.fori_loop(0, NZ, batch, 0)

    total = acc[HEAD : HEAD + 1, :]
    seen = total > 0.0
    safe = jnp.where(seen, total, 1.0)
    lse = jnp.where(seen, top[...] * SCALE2 + jnp.log2(safe), FAR)
    inverse = 1.0 / safe
    for n in range(NXY):
        cols = slice(n * 2 * ROWS, (n + 1) * 2 * ROWS)
        parts[n] = (acc[:HEAD, cols] * inverse[:, cols]).astype(BF16)
        levels[n] = jnp.broadcast_to(lse[:, cols], (8, 2 * ROWS))
    for n in others:
        copies["l", n].start()
        copies["o", n].start()
    held[x, y] = parts[x * NY + y]
    lses[x, y] = levels[x * NY + y]
    fetched[x] = pages[pl.ds(x * NY, NY)]
    load_wo.wait()
    for n in others:
        copies["l", n].wait_send()
        copies["o", n].wait_send()
    copies["p", 2].start()
    for n in others:
        copies["l", n].wait_recv()
        copies["o", n].wait_recv()
    for g in range(NY):
        rows = [lses[i, g, 0:1, :] for i in range(NX)]
        peak = jnp.maximum(jnp.maximum(rows[0], rows[1]), jnp.maximum(rows[2], rows[3]))
        shares = [jnp.exp2(row - peak) for row in rows]
        whole = shares[0] + shares[1] + shares[2] + shares[3]
        value = 0.0
        for i in range(NX):
            value += held[i, g].astype(F32) * (shares[i] / whole)
        for a in range(2):
            cols = slice((2 * g + a) * HEAD, (2 * g + a + 1) * HEAD)
            rows = jnp.transpose(value[:, a * ROWS : (a + 1) * ROWS].astype(BF16))
            context[0, :, cols] = rows[:BLOCK]
            context[1, :, cols] = rows[BLOCK:]

    theirs = context[partner]
    for n in range(CHUNKS):
        cols = slice(n * CHUNK, (n + 1) * CHUNK)
        outgoing[n] = jnp.dot(theirs, wo[:, cols], preferred_element_type=F32).astype(BF16)
        copies["t", n].start()
    ours = context[r]
    residual = tok[pl.ds(pl.multiple_of(r * BLOCK, BLOCK), BLOCK), :]
    for n in range(CHUNKS):
        cols = slice(n * CHUNK, (n + 1) * CHUNK)
        mine[:, cols] = residual[:, cols].astype(F32) + jnp.dot(
            ours, wo[:, cols], preferred_element_type=F32
        )
    for n in range(1, NX):
        copies["p", n].wait_recv()
    own_lanes = pl.ds(pl.multiple_of(y * HEAD, HEAD), HEAD)
    other_lanes = pl.ds(pl.multiple_of((1 - y) * HEAD, HEAD), HEAD)

    def chosen_page(to_y, j):
        at = table[1, (x * NY + to_y) * SLOTS + j]
        here = jnp.full((2, PAGE, HEAD), at, jnp.int32) >= 0
        return jnp.where(here, fetched[jnp.maximum(at, 0), to_y, j].astype(F32), 0.0).astype(BF16)

    for j in range(SLOTS):
        swapped[j] = chosen_page(1 - y, j)
    copies["w", 0].start()
    for j in range(SLOTS):
        cache_ref[j, :, :, own_lanes] = chosen_page(y, j)
    for n in range(CHUNKS):
        cols = slice(n * CHUNK, (n + 1) * CHUNK)
        copies["t", n].wait_recv()
        out_ref[:, cols] = (mine[:, cols] + incoming[n].astype(F32)).astype(BF16)
    copies["w", 0].wait_recv()
    for j in range(SLOTS):
        cache_ref[j, :, :, other_lanes] = swapping[j]
    for name, copy in copies.items():
        if name[0] not in ("l", "o"):
            copy.wait_send()


COPIES = 15 + 16 + 3 * (NXY - 1) + NX - 1 + CHUNKS + 1


def on_device(
    tokens, norm_gain, w_query, key_projection, value_projection, w_out, lengths, block_split, page_slot
):
    return pl.pallas_call(
        layer_kernel,
        out_shape=(
            jax.ShapeDtypeStruct((BLOCK, WIDTH), BF16),
            jax.ShapeDtypeStruct((SLOTS, 2, PAGE, KCOLS), BF16),
        ),
        in_specs=[SMEM, SMEM, SMEM, HBM, VMEM, HBM, HBM, HBM, HBM, VMEM],
        out_specs=(VMEM, VMEM),
        scratch_shapes=[
            pltpu.VMEM((ROWS, WIDTH), BF16),
            pltpu.VMEM((WIDTH, QCOLS), BF16),
            pltpu.VMEM((WIDTH, KCOLS), BF16),
            pltpu.VMEM((WIDTH, KCOLS), BF16),
            pltpu.VMEM((QCOLS, WIDTH), BF16),
            pltpu.VMEM((ROWS, WIDTH), BF16),
            pltpu.VMEM((ROWS, 1024), F32),
            pltpu.VMEM((2, 2, 4, PAGE, HEAD), BF16),
            pltpu.VMEM((2, 2, ROWS, HEAD), BF16),
            pltpu.VMEM((NZ, NC, NY, 2, 4, PAGE, HEAD), BF16),
            pltpu.VMEM((NX, NY, 2, ROWS, HEAD), BF16),
            pltpu.VMEM((HEAD + EXTRA, KEYS), BF16),
            pltpu.VMEM((HEAD + EXTRA, LANES), F32),
            pltpu.VMEM((1, LANES), F32),
            pltpu.VMEM((NXY, HEAD, 2 * ROWS), BF16),
            pltpu.VMEM((NXY, 8, 2 * ROWS), F32),
            pltpu.VMEM((NX, NY, HEAD, 2 * ROWS), BF16),
            pltpu.VMEM((NX, NY, 8, 2 * ROWS), F32),
            pltpu.VMEM((NXY, SLOTS, 2, PAGE, HEAD), BF16),
            pltpu.VMEM((NX, NY, SLOTS, 2, PAGE, HEAD), BF16),
            pltpu.VMEM((SLOTS, 2, PAGE, HEAD), BF16),
            pltpu.VMEM((SLOTS, 2, PAGE, HEAD), BF16),
            pltpu.VMEM((2, BLOCK, QCOLS), BF16),
            pltpu.VMEM((BLOCK, WIDTH), F32),
            pltpu.VMEM((CHUNKS, BLOCK, CHUNK), BF16),
            pltpu.VMEM((CHUNKS, BLOCK, CHUNK), BF16),
            pltpu.SemaphoreType.DMA((14,)),
            pltpu.SemaphoreType.DMA((COPIES,)),
            pltpu.SemaphoreType.DMA((COPIES,)),
        ],
        compiler_params=pltpu.CompilerParams(
            collective_id=1, has_side_effects=True, vmem_limit_bytes=54 * MIB
        ),
        name="layer",
    )(
        lengths, block_split, make_table(block_split, page_slot), tokens, norm_gain.reshape(1, WIDTH), w_query,
        key_projection, value_projection, w_out, jnp.asarray(FREQ),
    )


def solution(mesh):
    in_specs = (
        P("seq", None),
        P(),
        P(None, "req"),
        P(None, "req"),
        P(None, "req"),
        P("req", None),
        P(),
        P(),
        P(),
    )
    out_specs = (P(("seq", "req"), None), P("seq", None, None, "req"))
    return jax.shard_map(
        on_device, mesh=mesh, in_specs=in_specs, out_specs=out_specs, check_vma=False
    )
```

```python
import math

import jax
import jax.numpy as jnp
import numpy as np
from jax import lax
from jax.experimental import pallas as pl
from jax.experimental.pallas import tpu as pltpu
from jax.sharding import PartitionSpec as P

MESH = pl.DeviceIdType.MESH
ANY = pl.BlockSpec(memory_space=pl.ANY)
HBM = pl.BlockSpec(memory_space=pltpu.HBM)
VMEM = pl.BlockSpec(memory_space=pltpu.VMEM)
SMEM = pl.BlockSpec(memory_space=pltpu.SMEM)

NY, NX, NZ, NC = 2, 4, 8, 2
NSEQ = NY * NX * NZ * NC
NXY = NX * NY
HEAD = 128
BLOCK = 64
ROWS = 128
PAGE = 32
SLOTS = 8
WIDTH = 2048
QCOLS = 512
KCOLS = 256
THETA = 1000000.0
EPS = 1e-05
FAR = -1e30
FLOOR = -1e29
SCALE2 = math.log2(math.e) / math.sqrt(HEAD)
MIB = 1 << 20
BF16 = jnp.bfloat16
F32 = jnp.float32

EXTRA = 16
KEYS = NC * NY * ROWS
LANES = NXY * 2 * ROWS
BEYOND = 1 << 14
CHUNK = 512
CHUNKS = WIDTH // CHUNK

FREQ = np.power(
    np.float32(THETA), -(np.arange(HEAD // 2, dtype=np.float32) * np.float32(2.0 / HEAD))
).astype(np.float32)
FREQ = np.concatenate([FREQ, FREQ])[None, :]


def coords(d):
    return d // 64, (d // 16) % NX, (d // 2) % NZ, d % 2


def index_of(y, x, z, c):
    return ((y * NX + x) * NZ + z) * NC + c


def plane(y, x, z, c):
    return [
        ((x + i) % NX, y if j == 0 else 1 - y, index_of(y if j == 0 else 1 - y, (x + i) % NX, z, c))
        for j in range(NY)
        for i in range(NX)
    ]


def prompt_start(pos, begins):
    first = jnp.zeros_like(pos)
    for begin in begins:
        first = jnp.where(pos >= begin, begin, first)
    return first


def begins_of(lengths):
    one = lengths[0]
    two = one + lengths[1]
    return one, two, two + lengths[2]


def rotation(own, begins, freq):
    row = lax.broadcasted_iota(jnp.int32, (ROWS, HEAD), 0)
    pos = jnp.where(
        row < BLOCK, own * BLOCK + row, (2 * NSEQ - 1 - own) * BLOCK + row - BLOCK
    )
    angle = (pos - prompt_start(pos, begins)).astype(F32) * freq
    turns = jnp.floor(angle * (2.0 / math.pi) + 0.5)
    rest = angle - turns * 1.5703125
    rest = rest - turns * 4.837512969970703125e-4
    rest = rest - turns * 7.54978995489188216e-8
    quarter = turns.astype(jnp.int32) & 3
    sq = rest * rest
    sine = rest + rest * sq * (-1.6666654611e-1 + sq * (8.3321608736e-3 - sq * 1.9515295891e-4))
    cosine = (
        1.0
        - 0.5 * sq
        + sq * sq * (4.166664568298827e-2 + sq * (-1.388731625493765e-3 + sq * 2.443315711809948e-5))
    )
    odd = (quarter & 1) == 1
    turned_sine = jnp.where(odd, cosine, sine)
    turned_cosine = jnp.where(odd, sine, cosine)
    lower = lax.broadcasted_iota(jnp.int32, (ROWS, HEAD), 1) < HEAD // 2
    minus = (quarter >= 2) != lower
    sine = jnp.where(minus, -turned_sine, turned_sine)
    cosine = jnp.where((quarter == 1) | (quarter == 2), -turned_cosine, turned_cosine)
    return cosine, sine


def diagonal():
    return lax.broadcasted_iota(jnp.int32, (HEAD, HEAD), 0) == lax.broadcasted_iota(
        jnp.int32, (HEAD, HEAD), 1
    )


def stand(row, eye):
    return jnp.sum(jnp.where(eye, jnp.broadcast_to(row, (HEAD, HEAD)), 0.0), 1, keepdims=True)


def table_kernel(split_ref, slot_ref, table_ref):
    y, x, z, c = coords(lax.axis_index("seq"))
    eye = diagonal()
    sub = lax.broadcasted_iota(jnp.int32, (HEAD, HEAD), 0)
    row_lane = lax.broadcasted_iota(jnp.int32, (1, HEAD), 1)

    def pick(mask, value):
        return jnp.sum(jnp.where(mask, value, 0.0), 0, keepdims=True)

    ys, xs, zs, cs = coords(sub)
    split_col = jnp.broadcast_to(stand(split_ref[...].astype(F32), eye), (HEAD, HEAD))
    halves = (split_col, 2 * NSEQ - 1 - split_col)
    place = row_lane // SLOTS % NXY
    wanted = index_of(place % NY, place // NY, z, c) * SLOTS + row_lane % SLOTS
    page, found = 0.0, 0.0
    for k in range(4):
        slots = jnp.broadcast_to(stand(slot_ref[k : k + 1, :].astype(F32), eye), (HEAD, HEAD))
        hit = slots == wanted.astype(F32)
        page += pick(hit, (sub + HEAD * k).astype(F32))
        found += pick(hit, 1.0)
    page = page.astype(jnp.int32)
    block = (page // 2).astype(F32)
    at, column = 0.0, 0.0
    for h in range(2):
        hit = halves[h] == block
        at += pick(hit & (xs == x), (2 * ((zs * NC + cs) * NY + ys) + h).astype(F32))
        column += pick(hit, xs.astype(F32))
    table_ref[0:1, :] = at.astype(jnp.int32) * 2 + page % 2
    table_ref[1:2, :] = jnp.where(found > 0.5, column, -1.0).astype(jnp.int32)
    table_ref[2:, :] = jnp.zeros((6, HEAD), jnp.int32)


def make_table(block_split, page_slot):
    return pl.pallas_call(
        table_kernel,
        out_shape=jax.ShapeDtypeStruct((8, HEAD), jnp.int32),
        in_specs=[VMEM, VMEM],
        out_specs=VMEM,
        name="table",
    )(block_split.reshape(1, NSEQ), page_slot.reshape(4, HEAD))


NODES = [(0, 0)]
for _k in (1, 2, 3):
    NODES += [(1, -_k), (1, _k), (0, -_k), (0, _k)]
NODES += [(1, 4), (0, 4)]
PLACES = [(own, dz) for own in (1, 0) for dz in (0, -1, 1, -2, 2, -3, 3, 4)]


def passed_on(own, dz):
    out = []
    if -3 < dz <= 0 or (dz == -3 and own):
        out.append(("up", dz - 1))
    if 0 <= dz < 3 or (dz == 3 and not own):
        out.append(("down", dz + 1))
    return [(to, 4 if abs(to_dz) == 4 else to_dz) for to, to_dz in out]


def layer_kernel(
    lengths, split, table, tok_hbm, gain_ref, wq_hbm, wk_hbm, wv_hbm, wo_hbm, freq_ref,
    out_ref, cache_ref,
    tok, wq, wk, wv, wo, normed, proj, kv, q, kvall, qall, turned, acc, top,
    parts, levels, held, lses, pages, fetched, swapped, swapping, context, mine, outgoing, incoming,
    load_sem, send_sem, recv_sem,
):
    d, r = lax.axis_index("seq"), lax.axis_index("req")
    y, x, z, c = coords(d)
    partner = 1 - r
    loads = [pltpu.make_async_copy(tok_hbm, tok, load_sem.at[0])]
    for k in range(4):
        rows = pl.ds(512 * k, 512)
        for n, (src, dst) in enumerate(((wq_hbm, wq), (wk_hbm, wk), (wv_hbm, wv))):
            loads.append(
                pltpu.make_async_copy(src.at[rows], dst.at[rows], load_sem.at[1 + 3 * k + n])
            )
    load_wo = pltpu.make_async_copy(wo_hbm, wo, load_sem.at[13])
    for copy in loads + [load_wo]:
        copy.start()
    near = {
        "sib": (index_of(y, x, z, 1 - c), r),
        "up": (index_of(y, x, (z + 1) % NZ, c), r),
        "down": (index_of(y, x, (z + NZ - 1) % NZ, c), r),
        "req": (d, partner),
    }
    peers = plane(y, x, z, c)
    barrier = pltpu.get_barrier_semaphore()
    everyone = list(near.values()) + [(peer[2], r) for peer in peers[1:]]
    for peer in everyone:
        pl.semaphore_signal(barrier, inc=1, device_id=peer, device_id_type=MESH)

    copies = {}

    def plan(name, src, dst, to):
        n = len(copies)
        copies[name] = pltpu.make_async_remote_copy(
            src_ref=src,
            dst_ref=dst,
            send_sem=send_sem.at[n],
            recv_sem=recv_sem.at[n],
            device_id=to,
            device_id_type=MESH,
        )

    def shard(own, dz):
        return kvall.at[(z + dz + NZ) % NZ, c, y if own else 1 - y]

    plan((0, 0), kv.at[1 - y], shard(1, 0), (peers[NX][2], r))
    for own, dz in PLACES:
        for to, far in passed_on(own, dz):
            plan((own, far), shard(own, dz), shard(own, dz), near[to])
        plan(("s", own, dz), shard(own, dz), shard(own, dz), near["sib"])
    for n, (px, py, peer) in enumerate(peers):
        if n:
            to = (peer, r)
            plan(("q", n), q.at[py], qall.at[x, y], to)
            plan(("l", n), levels.at[px * NY + py], lses.at[x, y], to)
            plan(("o", n), parts.at[px * NY + py], held.at[x, y], to)
            if n < NX:
                plan(("p", n), pages.at[pl.ds(px * NY, NY)], fetched.at[x], to)
    for n in range(CHUNKS):
        plan(("t", n), outgoing.at[n], incoming.at[n], near["req"])
    plan(("w", 0), swapped, swapping, (peers[NX][2], r))
    others = range(1, NXY)

    def relay(*nodes):
        for own, dz in nodes:
            if (own, dz) != (1, 0):
                copies[own, dz].wait_recv()
            for _, far in passed_on(own, dz):
                copies[own, far].start()
            copies["s", own, dz].start()

    begins = begins_of(lengths)
    cosine, sine = rotation(split[d], begins, freq_ref[...])
    loads[0].wait()
    wide = tok[...].astype(F32)
    inv = lax.rsqrt(jnp.mean(wide * wide, -1, keepdims=True) + EPS)
    normed[...] = (wide * inv * gain_ref[...]).astype(BF16)
    for k in range(4):
        for copy in loads[1 + 3 * k : 4 + 3 * k]:
            copy.wait()
        rows = slice(512 * k, 512 * (k + 1))
        part = normed[:, rows]
        for cols, weights in ((slice(0, 512), wq), (slice(512, 768), wk), (slice(768, 1024), wv)):
            value = jnp.dot(part, weights[rows, :], preferred_element_type=F32)
            if k == 0:
                proj[:, cols] = value
            else:
                proj[:, cols] += value
    for h in range(6):
        u = proj[:, HEAD * h : HEAD * (h + 1)]
        rotated = (u * cosine + pltpu.roll(u, HEAD // 2, 1) * sine).astype(BF16)
        if h < 4:
            q[h // 2, h % 2] = rotated
        else:
            kv[h - 4, 0] = rotated.reshape(4, PAGE, HEAD)
    for g in range(2):
        kv[g, 1] = proj[:, 768 + HEAD * g : 768 + HEAD * (g + 1)].astype(BF16).reshape(4, PAGE, HEAD)
    kvall[z, c, y] = kv[y]
    qall[x, y] = q[y]
    pl.semaphore_wait(barrier, len(everyone))
    relay((1, 0))
    copies[0, 0].start()
    for n in others:
        copies["q", n].start()

    lane = lax.broadcasted_iota(jnp.int32, (1, ROWS), 1)
    pos = []
    for px in range(NX):
        for py in range(NY):
            block = split[index_of(py, px, z, c)]
            row = jnp.where(
                lane < BLOCK, block * BLOCK + lane, (2 * NSEQ - 1 - block) * BLOCK + lane - BLOCK
            )
            pos += [row, row]
    pos = jnp.concatenate(pos, 1)
    first = prompt_start(pos, begins)
    turned[HEAD:, :] = jnp.ones((EXTRA, KEYS), BF16)
    top[...] = jnp.full_like(top, FLOOR)
    acc[...] = jnp.zeros_like(acc)
    inner = lax.broadcasted_iota(jnp.int32, (BLOCK, LANES), 0)

    def build_pages():
        def one(n, _):
            at = table[0, n]
            for part in range(2):
                pages[n // SLOTS, n % SLOTS, part] = kvall[
                    at // 16, at // 8 % 2, at // 4 % 2, part, at % 4
                ]
            return 0

        lax.fori_loop(0, NXY * SLOTS, one, 0, unroll=8)

    def sibling(*places):
        for own, dz in places:
            copies["s", own, dz].wait_recv()

    def batch(i, _):
        @pl.when(i == 0)
        def _():
            relay((0, 0), (1, -1), (1, 1))
            relay((1, -2), (1, 2), (0, -1), (0, 1))
            sibling((1, 0), (0, 0))
            for n in others:
                copies["q", n].wait_recv()

        @pl.when(i == 1)
        def _():
            sibling((1, -1), (0, -1))

        @pl.when(i == 2)
        def _():
            relay((1, -3), (1, 3), (0, -2), (0, 2))
            sibling((1, 1), (0, 1))

        @pl.when(i == 3)
        def _():
            sibling((1, -2), (0, -2))

        @pl.when(i == 4)
        def _():
            relay((1, 4), (0, -3), (0, 3))
            sibling((1, 2), (0, 2))

        @pl.when(i == 5)
        def _():
            sibling((1, -3), (0, -3))

        @pl.when(i == 6)
        def _():
            relay((0, 4))
            sibling((1, 3), (0, 3))

        @pl.when(i == 7)
        def _():
            sibling((1, 4), (0, 4))

        half = (i + 1) // 2
        far = (z + NZ + half * (1 - i % 2 * 2)) % NZ
        pieces = [(cc, yy) for cc in range(NC) for yy in range(NY)]
        for n, (cc, yy) in enumerate(pieces):
            turned[:HEAD, n * ROWS : (n + 1) * ROWS] = jnp.transpose(
                kvall[far, cc, yy, 1].reshape(ROWS, HEAD)
            )
        keys = jnp.concatenate([kvall[far, cc, yy, 0].reshape(ROWS, HEAD) for cc, yy in pieces], 0)
        queries = qall[...].reshape(LANES, HEAD)
        s = lax.dot_general(keys, queries, (((1,), (1,)), ((), ())), preferred_element_type=F32)
        masked = []
        for n, (cc, yy) in enumerate(pieces):
            block = split[index_of(yy, x, far, cc)]
            for h in range(2):
                base = (block if h == 0 else 2 * NSEQ - 1 - block) * BLOCK
                visible = (inner >= first - base) & (inner <= pos - base)
                at = n * ROWS + h * BLOCK
                masked.append(jnp.where(visible, s[at : at + BLOCK], FAR))
        s = jnp.concatenate(masked, 0)
        before = top[...]
        higher = jnp.maximum(before, jnp.max(s, 0, keepdims=True))
        e = jnp.exp2((s - higher) * SCALE2).astype(BF16)
        fade = jnp.exp2((before - higher) * SCALE2)
        top[...] = higher
        acc[...] = acc[...] * fade + jnp.dot(turned[...], e, preferred_element_type=F32)
        return 0

    lax.fori_loop(0, NZ, batch, 0)

    total = acc[HEAD : HEAD + 1, :]
    seen = total > 0.0
    safe = jnp.where(seen, total, 1.0)
    lse = jnp.where(seen, top[...] * SCALE2 + jnp.log2(safe), FAR)
    inverse = 1.0 / safe
    for n in range(NXY):
        cols = slice(n * 2 * ROWS, (n + 1) * 2 * ROWS)
        parts[n] = (acc[:HEAD, cols] * inverse[:, cols]).astype(BF16)
        levels[n] = jnp.broadcast_to(lse[:, cols], (8, 2 * ROWS))
    for n in others:
        copies["l", n].start()
        copies["o", n].start()
    build_pages()
    for n in range(1, NX):
        copies["p", n].start()
    held[x, y] = parts[x * NY + y]
    lses[x, y] = levels[x * NY + y]
    fetched[x] = pages[pl.ds(x * NY, NY)]
    load_wo.wait()
    for n in others:
        copies["l", n].wait_send()
        copies["o", n].wait_send()
    for n in others:
        copies["l", n].wait_recv()
        copies["o", n].wait_recv()
    for g in range(NY):
        rows = [lses[i, g, 0:1, :] for i in range(NX)]
        peak = jnp.maximum(jnp.maximum(rows[0], rows[1]), jnp.maximum(rows[2], rows[3]))
        shares = [jnp.exp2(row - peak) for row in rows]
        whole = shares[0] + shares[1] + shares[2] + shares[3]
        value = 0.0
        for i in range(NX):
            value += held[i, g].astype(F32) * (shares[i] / whole)
        for a in range(2):
            cols = slice((2 * g + a) * HEAD, (2 * g + a + 1) * HEAD)
            rows = jnp.transpose(value[:, a * ROWS : (a + 1) * ROWS].astype(BF16))
            context[0, :, cols] = rows[:BLOCK]
            context[1, :, cols] = rows[BLOCK:]

    theirs = context[partner]
    for n in range(CHUNKS):
        cols = slice(n * CHUNK, (n + 1) * CHUNK)
        outgoing[n] = jnp.dot(theirs, wo[:, cols], preferred_element_type=F32).astype(BF16)
        copies["t", n].start()
    ours = context[r]
    residual = tok[pl.ds(pl.multiple_of(r * BLOCK, BLOCK), BLOCK), :]
    for n in range(CHUNKS):
        cols = slice(n * CHUNK, (n + 1) * CHUNK)
        mine[:, cols] = residual[:, cols].astype(F32) + jnp.dot(
            ours, wo[:, cols], preferred_element_type=F32
        )
    for n in range(1, NX):
        copies["p", n].wait_recv()
    own_lanes = pl.ds(pl.multiple_of(y * HEAD, HEAD), HEAD)
    other_lanes = pl.ds(pl.multiple_of((1 - y) * HEAD, HEAD), HEAD)

    def chosen_page(to_y, j):
        at = table[1, (x * NY + to_y) * SLOTS + j]
        here = jnp.full((2, PAGE, HEAD), at, jnp.int32) >= 0
        return jnp.where(here, fetched[jnp.maximum(at, 0), to_y, j].astype(F32), 0.0).astype(BF16)

    for j in range(SLOTS):
        swapped[j] = chosen_page(1 - y, j)
    copies["w", 0].start()
    for j in range(SLOTS):
        cache_ref[j, :, :, own_lanes] = chosen_page(y, j)
    for n in range(CHUNKS):
        cols = slice(n * CHUNK, (n + 1) * CHUNK)
        copies["t", n].wait_recv()
        out_ref[:, cols] = (mine[:, cols] + incoming[n].astype(F32)).astype(BF16)
    copies["w", 0].wait_recv()
    for j in range(SLOTS):
        cache_ref[j, :, :, other_lanes] = swapping[j]
    for name, copy in copies.items():
        if name[0] not in ("l", "o"):
            copy.wait_send()


COPIES = 15 + 16 + 3 * (NXY - 1) + NX - 1 + CHUNKS + 1


def on_device(
    tokens, norm_gain, w_query, key_projection, value_projection, w_out, lengths, block_split, page_slot
):
    return pl.pallas_call(
        layer_kernel,
        out_shape=(
            jax.ShapeDtypeStruct((BLOCK, WIDTH), BF16),
            jax.ShapeDtypeStruct((SLOTS, 2, PAGE, KCOLS), BF16),
        ),
        in_specs=[SMEM, SMEM, SMEM, HBM, VMEM, HBM, HBM, HBM, HBM, VMEM],
        out_specs=(VMEM, VMEM),
        scratch_shapes=[
            pltpu.VMEM((ROWS, WIDTH), BF16),
            pltpu.VMEM((WIDTH, QCOLS), BF16),
            pltpu.VMEM((WIDTH, KCOLS), BF16),
            pltpu.VMEM((WIDTH, KCOLS), BF16),
            pltpu.VMEM((QCOLS, WIDTH), BF16),
            pltpu.VMEM((ROWS, WIDTH), BF16),
            pltpu.VMEM((ROWS, 1024), F32),
            pltpu.VMEM((2, 2, 4, PAGE, HEAD), BF16),
            pltpu.VMEM((2, 2, ROWS, HEAD), BF16),
            pltpu.VMEM((NZ, NC, NY, 2, 4, PAGE, HEAD), BF16),
            pltpu.VMEM((NX, NY, 2, ROWS, HEAD), BF16),
            pltpu.VMEM((HEAD + EXTRA, KEYS), BF16),
            pltpu.VMEM((HEAD + EXTRA, LANES), F32),
            pltpu.VMEM((1, LANES), F32),
            pltpu.VMEM((NXY, HEAD, 2 * ROWS), BF16),
            pltpu.VMEM((NXY, 8, 2 * ROWS), F32),
            pltpu.VMEM((NX, NY, HEAD, 2 * ROWS), BF16),
            pltpu.VMEM((NX, NY, 8, 2 * ROWS), F32),
            pltpu.VMEM((NXY, SLOTS, 2, PAGE, HEAD), BF16),
            pltpu.VMEM((NX, NY, SLOTS, 2, PAGE, HEAD), BF16),
            pltpu.VMEM((SLOTS, 2, PAGE, HEAD), BF16),
            pltpu.VMEM((SLOTS, 2, PAGE, HEAD), BF16),
            pltpu.VMEM((2, BLOCK, QCOLS), BF16),
            pltpu.VMEM((BLOCK, WIDTH), F32),
            pltpu.VMEM((CHUNKS, BLOCK, CHUNK), BF16),
            pltpu.VMEM((CHUNKS, BLOCK, CHUNK), BF16),
            pltpu.SemaphoreType.DMA((14,)),
            pltpu.SemaphoreType.DMA((COPIES,)),
            pltpu.SemaphoreType.DMA((COPIES,)),
        ],
        compiler_params=pltpu.CompilerParams(
            collective_id=1, has_side_effects=True, vmem_limit_bytes=54 * MIB
        ),
        name="layer",
    )(
        lengths, block_split, make_table(block_split, page_slot), tokens, norm_gain.reshape(1, WIDTH), w_query,
        key_projection, value_projection, w_out, jnp.asarray(FREQ),
    )


def solution(mesh):
    in_specs = (
        P("seq", None),
        P(),
        P(None, "req"),
        P(None, "req"),
        P(None, "req"),
        P("req", None),
        P(),
        P(),
        P(),
    )
    out_specs = (P(("seq", "req"), None), P("seq", None, None, "req"))
    return jax.shard_map(
        on_device, mesh=mesh, in_specs=in_specs, out_specs=out_specs, check_vma=False
    )
```

```python
import math

import jax
import jax.numpy as jnp
import numpy as np
from jax import lax
from jax.experimental import pallas as pl
from jax.experimental.pallas import tpu as pltpu
from jax.sharding import PartitionSpec as P

MESH = pl.DeviceIdType.MESH
ANY = pl.BlockSpec(memory_space=pl.ANY)
HBM = pl.BlockSpec(memory_space=pltpu.HBM)
VMEM = pl.BlockSpec(memory_space=pltpu.VMEM)
SMEM = pl.BlockSpec(memory_space=pltpu.SMEM)

NY, NX, NZ, NC = 2, 4, 8, 2
NSEQ = NY * NX * NZ * NC
NXY = NX * NY
HEAD = 128
BLOCK = 64
ROWS = 128
PAGE = 32
SLOTS = 8
WIDTH = 2048
QCOLS = 512
KCOLS = 256
THETA = 1000000.0
EPS = 1e-05
FAR = -1e30
FLOOR = -1e29
SCALE2 = math.log2(math.e) / math.sqrt(HEAD)
MIB = 1 << 20
BF16 = jnp.bfloat16
F32 = jnp.float32

EXTRA = 16
KEYS = NC * NY * ROWS
LANES = NXY * 2 * ROWS
BEYOND = 1 << 14
CHUNK = 512
CHUNKS = WIDTH // CHUNK

FREQ = np.power(
    np.float32(THETA), -(np.arange(HEAD // 2, dtype=np.float32) * np.float32(2.0 / HEAD))
).astype(np.float32)
FREQ = np.concatenate([FREQ, FREQ])[None, :]


def coords(d):
    return d // 64, (d // 16) % NX, (d // 2) % NZ, d % 2


def index_of(y, x, z, c):
    return ((y * NX + x) * NZ + z) * NC + c


def plane(y, x, z, c):
    return [
        ((x + i) % NX, y if j == 0 else 1 - y, index_of(y if j == 0 else 1 - y, (x + i) % NX, z, c))
        for j in range(NY)
        for i in range(NX)
    ]


def prompt_start(pos, begins):
    first = jnp.zeros_like(pos)
    for begin in begins:
        first = jnp.where(pos >= begin, begin, first)
    return first


def begins_of(lengths):
    one = lengths[0]
    two = one + lengths[1]
    return one, two, two + lengths[2]


def rotation(own, begins, freq):
    row = lax.broadcasted_iota(jnp.int32, (ROWS, HEAD), 0)
    pos = jnp.where(
        row < BLOCK, own * BLOCK + row, (2 * NSEQ - 1 - own) * BLOCK + row - BLOCK
    )
    angle = (pos - prompt_start(pos, begins)).astype(F32) * freq
    turns = jnp.floor(angle * (2.0 / math.pi) + 0.5)
    rest = angle - turns * 1.5703125
    rest = rest - turns * 4.837512969970703125e-4
    rest = rest - turns * 7.54978995489188216e-8
    quarter = turns.astype(jnp.int32) & 3
    sq = rest * rest
    sine = rest + rest * sq * (-1.6666654611e-1 + sq * (8.3321608736e-3 - sq * 1.9515295891e-4))
    cosine = (
        1.0
        - 0.5 * sq
        + sq * sq * (4.166664568298827e-2 + sq * (-1.388731625493765e-3 + sq * 2.443315711809948e-5))
    )
    odd = (quarter & 1) == 1
    turned_sine = jnp.where(odd, cosine, sine)
    turned_cosine = jnp.where(odd, sine, cosine)
    lower = lax.broadcasted_iota(jnp.int32, (ROWS, HEAD), 1) < HEAD // 2
    minus = (quarter >= 2) != lower
    sine = jnp.where(minus, -turned_sine, turned_sine)
    cosine = jnp.where((quarter == 1) | (quarter == 2), -turned_cosine, turned_cosine)
    return cosine, sine


def diagonal():
    return lax.broadcasted_iota(jnp.int32, (HEAD, HEAD), 0) == lax.broadcasted_iota(
        jnp.int32, (HEAD, HEAD), 1
    )


def stand(row, eye):
    return jnp.sum(jnp.where(eye, jnp.broadcast_to(row, (HEAD, HEAD)), 0.0), 1, keepdims=True)


def make_table(table_ref, split_ref, slot_ref, y, x, z, c):
    eye = diagonal()
    sub = lax.broadcasted_iota(jnp.int32, (HEAD, HEAD), 0)
    row_lane = lax.broadcasted_iota(jnp.int32, (1, HEAD), 1)

    def pick(mask, value):
        return jnp.sum(jnp.where(mask, value, 0), 0, keepdims=True)

    def upright(row):
        return jnp.broadcast_to(
            jnp.sum(jnp.where(eye, jnp.broadcast_to(row, (HEAD, HEAD)), 0), 1, keepdims=True), (HEAD, HEAD)
        )

    ys, xs, zs, cs = coords(sub)
    split_col = upright(split_ref[...])
    halves = (split_col, 2 * NSEQ - 1 - split_col)
    place = row_lane // SLOTS % NXY
    wanted = index_of(place % NY, place // NY, z, c) * SLOTS + row_lane % SLOTS
    page, found = 0, 0
    for k in range(4):
        hit = upright(slot_ref[k : k + 1, :]) == wanted
        page += pick(hit, sub + HEAD * k)
        found += pick(hit, 1)
    block = page // 2
    at, column = 0, 0
    for h in range(2):
        hit = halves[h] == block
        at += pick(hit & (xs == x), 2 * ((zs * NC + cs) * NY + ys) + h)
        column += pick(hit, xs)
    table_ref[0:1, :] = jnp.minimum(at * 2 + page % 2, 2 * NSEQ // 2 - 1)
    table_ref[1:2, :] = jnp.where(found > 0, jnp.minimum(column, NX - 1), -1)
    table_ref[2:, :] = jnp.zeros((6, HEAD), jnp.int32)


NODES = [(0, 0)]
for _k in (1, 2, 3):
    NODES += [(1, -_k), (1, _k), (0, -_k), (0, _k)]
NODES += [(1, 4), (0, 4)]
PLACES = [(own, dz) for own in (1, 0) for dz in (0, -1, 1, -2, 2, -3, 3, 4)]


def passed_on(own, dz):
    out = []
    if -3 < dz <= 0 or (dz == -3 and own):
        out.append(("up", dz - 1))
    if 0 <= dz < 3 or (dz == 3 and not own):
        out.append(("down", dz + 1))
    return [(to, 4 if abs(to_dz) == 4 else to_dz) for to, to_dz in out]


def layer_kernel(
    lengths, split, tok_hbm, gain_ref, wq_hbm, wk_hbm, wv_hbm, wo_hbm, freq_ref, split_ref, slot_ref,
    out_ref, cache_ref,
    tok, wq, wk, wv, wo, normed, proj, kv, q, kvall, qall, turned, acc, top, table_v, table,
    parts, levels, held, lses, pages, fetched, swapped, swapping, context, mine, outgoing, incoming,
    load_sem, send_sem, recv_sem,
):
    d, r = lax.axis_index("seq"), lax.axis_index("req")
    y, x, z, c = coords(d)
    partner = 1 - r
    loads = [pltpu.make_async_copy(tok_hbm, tok, load_sem.at[0])]
    for k in range(4):
        rows = pl.ds(512 * k, 512)
        for n, (src, dst) in enumerate(((wq_hbm, wq), (wk_hbm, wk), (wv_hbm, wv))):
            loads.append(
                pltpu.make_async_copy(src.at[rows], dst.at[rows], load_sem.at[1 + 3 * k + n])
            )
    load_wo = pltpu.make_async_copy(wo_hbm, wo, load_sem.at[13])
    for copy in loads + [load_wo]:
        copy.start()
    near = {
        "sib": (index_of(y, x, z, 1 - c), r),
        "up": (index_of(y, x, (z + 1) % NZ, c), r),
        "down": (index_of(y, x, (z + NZ - 1) % NZ, c), r),
        "req": (d, partner),
    }
    peers = plane(y, x, z, c)
    barrier = pltpu.get_barrier_semaphore()
    everyone = list(near.values()) + [(peer[2], r) for peer in peers[1:]]
    for peer in everyone:
        pl.semaphore_signal(barrier, inc=1, device_id=peer, device_id_type=MESH)

    copies = {}

    def plan(name, src, dst, to):
        n = len(copies)
        copies[name] = pltpu.make_async_remote_copy(
            src_ref=src,
            dst_ref=dst,
            send_sem=send_sem.at[n],
            recv_sem=recv_sem.at[n],
            device_id=to,
            device_id_type=MESH,
        )

    def shard(own, dz):
        return kvall.at[(z + dz + NZ) % NZ, c, y if own else 1 - y]

    plan((0, 0), kv.at[1 - y], shard(1, 0), (peers[NX][2], r))
    for own, dz in PLACES:
        for to, far in passed_on(own, dz):
            plan((own, far), shard(own, dz), shard(own, dz), near[to])
        plan(("s", own, dz), shard(own, dz), shard(own, dz), near["sib"])
    for n, (px, py, peer) in enumerate(peers):
        if n:
            to = (peer, r)
            plan(("q", n), q.at[py], qall.at[x, y], to)
            plan(("l", n), levels.at[px * NY + py], lses.at[x, y], to)
            plan(("o", n), parts.at[px * NY + py], held.at[x, y], to)
            if n < NX:
                plan(("p", n), pages.at[pl.ds(px * NY, NY)], fetched.at[x], to)
    for n in range(CHUNKS):
        plan(("t", n), outgoing.at[n], incoming.at[n], near["req"])
    plan(("w", 0), swapped, swapping, (peers[NX][2], r))
    others = range(1, NXY)

    def relay(*nodes):
        for own, dz in nodes:
            if (own, dz) != (1, 0):
                copies[own, dz].wait_recv()
            for _, far in passed_on(own, dz):
                copies[own, far].start()
            copies["s", own, dz].start()

    begins = begins_of(lengths)
    cosine, sine = rotation(split[d], begins, freq_ref[...])
    loads[0].wait()
    wide = tok[...].astype(F32)
    inv = lax.rsqrt(jnp.mean(wide * wide, -1, keepdims=True) + EPS)
    normed[...] = (wide * inv * gain_ref[...]).astype(BF16)
    for k in range(4):
        for copy in loads[1 + 3 * k : 4 + 3 * k]:
            copy.wait()
        rows = slice(512 * k, 512 * (k + 1))
        part = normed[:, rows]
        for cols, weights in ((slice(0, 512), wq), (slice(512, 768), wk), (slice(768, 1024), wv)):
            value = jnp.dot(part, weights[rows, :], preferred_element_type=F32)
            if k == 0:
                proj[:, cols] = value
            else:
                proj[:, cols] += value
    for h in range(6):
        u = proj[:, HEAD * h : HEAD * (h + 1)]
        rotated = (u * cosine + pltpu.roll(u, HEAD // 2, 1) * sine).astype(BF16)
        if h < 4:
            q[h // 2, h % 2] = rotated
        else:
            kv[h - 4, 0] = rotated.reshape(4, PAGE, HEAD)
    for g in range(2):
        kv[g, 1] = proj[:, 768 + HEAD * g : 768 + HEAD * (g + 1)].astype(BF16).reshape(4, PAGE, HEAD)
    kvall[z, c, y] = kv[y]
    qall[x, y] = q[y]
    pl.semaphore_wait(barrier, len(everyone))
    relay((1, 0))
    copies[0, 0].start()
    for n in others:
        copies["q", n].start()

    make_table(table_v, split_ref, slot_ref, y, x, z, c)
    to_scalars = pltpu.make_async_copy(table_v, table, load_sem.at[14])
    to_scalars.start()
    lane = lax.broadcasted_iota(jnp.int32, (1, ROWS), 1)
    pos = []
    for px in range(NX):
        for py in range(NY):
            block = split[index_of(py, px, z, c)]
            row = jnp.where(
                lane < BLOCK, block * BLOCK + lane, (2 * NSEQ - 1 - block) * BLOCK + lane - BLOCK
            )
            pos += [row, row]
    pos = jnp.concatenate(pos, 1)
    first = prompt_start(pos, begins)
    turned[HEAD:, :] = jnp.ones((EXTRA, KEYS), BF16)
    top[...] = jnp.full_like(top, FLOOR)
    acc[...] = jnp.zeros_like(acc)
    inner = lax.broadcasted_iota(jnp.int32, (BLOCK, LANES), 0)
    to_scalars.wait()

    def build_pages():
        def one(n, _):
            at = table[0, n]
            for part in range(2):
                pages[n // SLOTS, n % SLOTS, part] = kvall[
                    at // 16, at // 8 % 2, at // 4 % 2, part, at % 4
                ]
            return 0

        lax.fori_loop(0, NXY * SLOTS, one, 0, unroll=8)

    def sibling(*places):
        for own, dz in places:
            copies["s", own, dz].wait_recv()

    def batch(i, _):
        @pl.when(i == 0)
        def _():
            relay((0, 0), (1, -1), (1, 1))
            relay((1, -2), (1, 2), (0, -1), (0, 1))
            sibling((1, 0), (0, 0))
            for n in others:
                copies["q", n].wait_recv()

        @pl.when(i == 1)
        def _():
            sibling((1, -1), (0, -1))

        @pl.when(i == 2)
        def _():
            relay((1, -3), (1, 3), (0, -2), (0, 2))
            sibling((1, 1), (0, 1))

        @pl.when(i == 3)
        def _():
            sibling((1, -2), (0, -2))

        @pl.when(i == 4)
        def _():
            relay((1, 4), (0, -3), (0, 3))
            sibling((1, 2), (0, 2))

        @pl.when(i == 5)
        def _():
            sibling((1, -3), (0, -3))

        @pl.when(i == 6)
        def _():
            relay((0, 4))
            sibling((1, 3), (0, 3))

        @pl.when(i == 7)
        def _():
            sibling((1, 4), (0, 4))

        half = (i + 1) // 2
        far = (z + NZ + half * (1 - i % 2 * 2)) % NZ
        pieces = [(cc, yy) for cc in range(NC) for yy in range(NY)]
        for n, (cc, yy) in enumerate(pieces):
            turned[:HEAD, n * ROWS : (n + 1) * ROWS] = jnp.transpose(
                kvall[far, cc, yy, 1].reshape(ROWS, HEAD)
            )
        keys = jnp.concatenate([kvall[far, cc, yy, 0].reshape(ROWS, HEAD) for cc, yy in pieces], 0)
        queries = qall[...].reshape(LANES, HEAD)
        s = lax.dot_general(keys, queries, (((1,), (1,)), ((), ())), preferred_element_type=F32)
        masked = []
        for n, (cc, yy) in enumerate(pieces):
            block = split[index_of(yy, x, far, cc)]
            for h in range(2):
                base = (block if h == 0 else 2 * NSEQ - 1 - block) * BLOCK
                visible = (inner >= first - base) & (inner <= pos - base)
                at = n * ROWS + h * BLOCK
                masked.append(jnp.where(visible, s[at : at + BLOCK], FAR))
        s = jnp.concatenate(masked, 0)
        before = top[...]
        higher = jnp.maximum(before, jnp.max(s, 0, keepdims=True))
        e = jnp.exp2((s - higher) * SCALE2).astype(BF16)
        fade = jnp.exp2((before - higher) * SCALE2)
        top[...] = higher
        acc[...] = acc[...] * fade + jnp.dot(turned[...], e, preferred_element_type=F32)
        return 0

    lax.fori_loop(0, NZ, batch, 0)

    total = acc[HEAD : HEAD + 1, :]
    seen = total > 0.0
    safe = jnp.where(seen, total, 1.0)
    top[...] = jnp.where(seen, top[...] * SCALE2 + jnp.log2(safe), FAR)
    acc[HEAD : HEAD + 1, :] = 1.0 / safe
    for n in list(others) + [0]:
        to = peers[n][0] * NY + peers[n][1]
        cols = pl.ds(pl.multiple_of(to * 2 * ROWS, 2 * ROWS), 2 * ROWS)
        levels[to] = jnp.broadcast_to(top[:, cols], (8, 2 * ROWS))
        parts[to] = (acc[:HEAD, cols] * acc[HEAD : HEAD + 1, cols]).astype(BF16)
        if n:
            copies["l", n].start()
            copies["o", n].start()
    build_pages()
    for n in range(1, NX):
        copies["p", n].start()
    held[x, y] = parts[x * NY + y]
    lses[x, y] = levels[x * NY + y]
    fetched[x] = pages[pl.ds(x * NY, NY)]
    load_wo.wait()
    for n in others:
        copies["l", n].wait_send()
        copies["o", n].wait_send()
    for n in others:
        copies["l", n].wait_recv()
        copies["o", n].wait_recv()
    for g in range(NY):
        rows = [lses[i, g, 0:1, :] for i in range(NX)]
        peak = jnp.maximum(jnp.maximum(rows[0], rows[1]), jnp.maximum(rows[2], rows[3]))
        shares = [jnp.exp2(row - peak) for row in rows]
        whole = shares[0] + shares[1] + shares[2] + shares[3]
        value = 0.0
        for i in range(NX):
            value += held[i, g].astype(F32) * (shares[i] / whole)
        for a in range(2):
            cols = slice((2 * g + a) * HEAD, (2 * g + a + 1) * HEAD)
            rows = jnp.transpose(value[:, a * ROWS : (a + 1) * ROWS].astype(BF16))
            context[0, :, cols] = rows[:BLOCK]
            context[1, :, cols] = rows[BLOCK:]

    theirs = context[partner]
    for n in range(CHUNKS):
        cols = slice(n * CHUNK, (n + 1) * CHUNK)
        outgoing[n] = jnp.dot(theirs, wo[:, cols], preferred_element_type=F32).astype(BF16)
        copies["t", n].start()
    ours = context[r]
    residual = tok[pl.ds(pl.multiple_of(r * BLOCK, BLOCK), BLOCK), :]
    for n in range(CHUNKS):
        cols = slice(n * CHUNK, (n + 1) * CHUNK)
        mine[:, cols] = residual[:, cols].astype(F32) + jnp.dot(
            ours, wo[:, cols], preferred_element_type=F32
        )
    for n in range(1, NX):
        copies["p", n].wait_recv()
    own_lanes = pl.ds(pl.multiple_of(y * HEAD, HEAD), HEAD)
    other_lanes = pl.ds(pl.multiple_of((1 - y) * HEAD, HEAD), HEAD)

    def chosen_page(to_y, j):
        at = table[1, (x * NY + to_y) * SLOTS + j]
        here = jnp.full((2, PAGE, HEAD), at, jnp.int32) >= 0
        return jnp.where(here, fetched[jnp.maximum(at, 0), to_y, j].astype(F32), 0.0).astype(BF16)

    for j in range(SLOTS):
        swapped[j] = chosen_page(1 - y, j)
    copies["w", 0].start()
    for j in range(SLOTS):
        cache_ref[j, :, :, own_lanes] = chosen_page(y, j)
    for n in range(CHUNKS):
        cols = slice(n * CHUNK, (n + 1) * CHUNK)
        copies["t", n].wait_recv()
        out_ref[:, cols] = (mine[:, cols] + incoming[n].astype(F32)).astype(BF16)
    copies["w", 0].wait_recv()
    for j in range(SLOTS):
        cache_ref[j, :, :, other_lanes] = swapping[j]
    for name, copy in copies.items():
        if name[0] not in ("l", "o"):
            copy.wait_send()


COPIES = 15 + 16 + 3 * (NXY - 1) + NX - 1 + CHUNKS + 1


def on_device(
    tokens, norm_gain, w_query, key_projection, value_projection, w_out, lengths, block_split, page_slot
):
    return pl.pallas_call(
        layer_kernel,
        out_shape=(
            jax.ShapeDtypeStruct((BLOCK, WIDTH), BF16),
            jax.ShapeDtypeStruct((SLOTS, 2, PAGE, KCOLS), BF16),
        ),
        in_specs=[SMEM, SMEM, HBM, VMEM, HBM, HBM, HBM, HBM, VMEM, VMEM, VMEM],
        out_specs=(VMEM, VMEM),
        scratch_shapes=[
            pltpu.VMEM((ROWS, WIDTH), BF16),
            pltpu.VMEM((WIDTH, QCOLS), BF16),
            pltpu.VMEM((WIDTH, KCOLS), BF16),
            pltpu.VMEM((WIDTH, KCOLS), BF16),
            pltpu.VMEM((QCOLS, WIDTH), BF16),
            pltpu.VMEM((ROWS, WIDTH), BF16),
            pltpu.VMEM((ROWS, 1024), F32),
            pltpu.VMEM((2, 2, 4, PAGE, HEAD), BF16),
            pltpu.VMEM((2, 2, ROWS, HEAD), BF16),
            pltpu.VMEM((NZ, NC, NY, 2, 4, PAGE, HEAD), BF16),
            pltpu.VMEM((NX, NY, 2, ROWS, HEAD), BF16),
            pltpu.VMEM((HEAD + EXTRA, KEYS), BF16),
            pltpu.VMEM((HEAD + EXTRA, LANES), F32),
            pltpu.VMEM((1, LANES), F32),
            pltpu.VMEM((8, HEAD), jnp.int32),
            pltpu.SMEM((8, HEAD), jnp.int32),
            pltpu.VMEM((NXY, HEAD, 2 * ROWS), BF16),
            pltpu.VMEM((NXY, 8, 2 * ROWS), F32),
            pltpu.VMEM((NX, NY, HEAD, 2 * ROWS), BF16),
            pltpu.VMEM((NX, NY, 8, 2 * ROWS), F32),
            pltpu.VMEM((NXY, SLOTS, 2, PAGE, HEAD), BF16),
            pltpu.VMEM((NX, NY, SLOTS, 2, PAGE, HEAD), BF16),
            pltpu.VMEM((SLOTS, 2, PAGE, HEAD), BF16),
            pltpu.VMEM((SLOTS, 2, PAGE, HEAD), BF16),
            pltpu.VMEM((2, BLOCK, QCOLS), BF16),
            pltpu.VMEM((BLOCK, WIDTH), F32),
            pltpu.VMEM((CHUNKS, BLOCK, CHUNK), BF16),
            pltpu.VMEM((CHUNKS, BLOCK, CHUNK), BF16),
            pltpu.SemaphoreType.DMA((15,)),
            pltpu.SemaphoreType.DMA((COPIES,)),
            pltpu.SemaphoreType.DMA((COPIES,)),
        ],
        compiler_params=pltpu.CompilerParams(
            collective_id=1, has_side_effects=True, vmem_limit_bytes=54 * MIB
        ),
        name="layer",
    )(
        lengths, block_split, tokens, norm_gain.reshape(1, WIDTH), w_query, key_projection, value_projection,
        w_out, jnp.asarray(FREQ), block_split.reshape(1, NSEQ), page_slot.reshape(4, HEAD),
    )


def solution(mesh):
    in_specs = (
        P("seq", None),
        P(),
        P(None, "req"),
        P(None, "req"),
        P(None, "req"),
        P("req", None),
        P(),
        P(),
        P(),
    )
    out_specs = (P(("seq", "req"), None), P("seq", None, None, "req"))
    return jax.shard_map(
        on_device, mesh=mesh, in_specs=in_specs, out_specs=out_specs, check_vma=False
    )
```
